512 devices in a mesh: sta: 16 (over z), grp: 8 (over y, core), hr: 4 (over x).
Axes of the slice: x: 4, y: 4, z: 16, core: 2. Of those that a mesh axis runs over, the one named last changes fastest.
Arguments:
- spectra: bfloat16 [4, 128, 6, 8192], P('hr', 'sta'), may hold values from -6 to 6
- pair_source: int32 [2048], P(('sta', 'grp')), may hold values from 0 to 7
- pair_owner: int32 [2048, 1], P(('sta', 'grp')), may hold values from 0 to 15; in each aligned block of 16 rows (0 to 15, 16 to 31, ...) at most 2 rows name the same one
- pair_row: int32 [2048], P(('sta', 'grp')), may hold values from 0 to 7
Outputs:
- stacked: float32 [2048, 9, 1024], P(('sta', 'grp'))
The draws below stay inside these ranges and needn't reach their ends.
Inputs may be any that keep to these rules, and one draw needn't show every extreme that they name: `pair_owner`: in each aligned block of 16 pairs (the pairs of one device) no value is named by more than 2 pairs, and in some block one value is named by exactly 2 pairs.
All inputs are finite; a program needn't handle non-finite values.
Results may differ from the reference program's by a relative error of at most 0.0032.
Values may be sent and summed in bfloat16 or wider, within the bound.
No kernel may reach another device: no remote copies, remote signals or barrier semaphores. Data moves between devices by JAX's collectives and lax.ppermute only.
A program may use at most 128 MiB of HBM per device.

```python
import math
import jax
import jax.numpy as jnp
import numpy as np
from jax import lax

BINS = 8192
LAGS = 1024
STA_DEV = 8
PAIR_DEV = 16
CAP = 2
STATIONS = 128
HOURS = 4
PAIRS = 2048
N_STA = 16
N_GRP = 8


def touch_ends(result, rng, least, top_value):
    spot = [jax.random.randint(jax.random.fold_in(rng, axis), (), 0, length) for axis, length in enumerate(result.shape)]
    main_axis = result.shape.index(max(result.shape))
    next_to = spot[:main_axis] + [(spot[main_axis] + 1) % result.shape[main_axis]] + spot[main_axis + 1:]
    return result.at[tuple(spot)].set(least).at[tuple(next_to)].set(top_value)


def levels(key, dims, cuts, smallest, top_value):
    def one(dim, shards_of):
        steps = jax.random.uniform(jax.random.fold_in(jax.random.fold_in(key, 6), dim), (shards_of,), jnp.float32, smallest / len(cuts), top_value / len(cuts))
        return jnp.repeat(jnp.exp(steps), dims[dim] // shards_of).reshape((-1,) + (1,) * (len(dims) - dim - 1))

    factor_of = one(*cuts[0])
    for cut in cuts[1:]:
        factor_of = factor_of * one(*cut)
    return factor_of


def shared_out(rng, own, number, rows, amount, top, bound, slope):
    order = jax.random.permutation(rng, amount)
    heavy_load, ordinary = portions_of(amount, rows * top, bound, slope, True), portions_of(amount, rows * top, bound, slope, False)
    places = jnp.arange(amount)

    def named(sizes, rotation):
        used = int((sizes > 0).sum())
        fixed = max(1, used // 4)
        moved = fixed + (places - fixed + rotation * (used - fixed)) % max(1, amount - fixed)
        return jnp.zeros((amount,), jnp.int32).at[order[jnp.where(places < fixed, places, moved)]].set(jnp.asarray(sizes, jnp.int32))

    sizes = jnp.where(number % 4 == 0, named(heavy_load, number // 4), named(ordinary, number - number // 4 - 1))
    mixed = jax.random.permutation(jax.random.fold_in(own, 3), amount)
    giver, taker = mixed[0:amount // 2 * 2:2], mixed[1:amount // 2 * 2:2]
    margin = jnp.minimum(sizes[giver] - 1, bound - sizes[taker]) // 2
    margin = jnp.where((giver == order[0]) | (taker == order[0]) | (sizes[taker] == 0), 0, jnp.maximum(margin, 0))
    moved = jax.random.randint(jax.random.fold_in(own, 4), (amount // 2,), 0, 1 << 20) % (margin + 1)
    sizes = sizes.at[giver].add(-moved).at[taker].add(moved)
    items = jnp.searchsorted(jnp.cumsum(sizes), jnp.arange(rows * top), side="right").astype(jnp.int32)
    listing = items.reshape(top, rows).T
    listing = listing[jax.random.permutation(jax.random.fold_in(own, 1), rows)]
    rotation = jax.random.randint(jax.random.fold_in(own, 2), (rows, 1), 0, top)
    return jnp.take_along_axis(listing, (jnp.arange(top)[None, :] + rotation) % top, axis=1)


def portions_of(count, total, reach, skew, full):
    portions = [(1 << 20) // math.isqrt(standing ** skew) + 1 for standing in range(1, count + 1)]
    largest = reach if full else min(reach, max(-(-total // count), total * portions[0] // sum(portions)))
    least = 1 if total - largest >= count - 1 else 0
    given, spare = [largest] + [least] * (count - 1), total - largest - least * (count - 1)
    while spare > 0:
        movable = [i for i in range(1, count) if given[i] < largest] or [i for i in range(1, count) if given[i] < reach]
        whole, left = sum([portions[i] for i in movable]), spare
        for i in movable:
            more = min(reach - given[i], max(1, left * portions[i] // whole), spare)
            given[i] = given[i] + more
            spare = spare - more
    return np.array(given)


def scatter_about(own_key, dims, width, reach, shards=(), kind=jnp.bfloat16):
    array = width * jax.random.normal(own_key, dims, jnp.float32)
    if shards:
        array = array * levels(own_key, dims, shards, -0.22, 0.18)
    return jnp.clip(array, -reach, reach).astype(kind)


def setup_inputs(seed: int = 0) -> dict:
    streams_of = jax.random.split(jax.random.key(seed), 5)
    spectra = scatter_about(streams_of[0], (HOURS, STATIONS, 6, BINS), 1.0, 6.0, ((0, 4), (1, 16)))
    pair_source = touch_ends(jax.random.randint(streams_of[1], (PAIRS,), 0, STA_DEV), jax.random.fold_in(streams_of[1], 1), 0, STA_DEV - 1).astype(jnp.int32)
    pair_owner_keys = jax.random.split(jax.random.fold_in(streams_of[2], 1), PAIRS // PAIR_DEV)
    pair_owner_turns = jax.random.permutation(jax.random.fold_in(streams_of[2], 3), PAIRS // PAIR_DEV)
    pair_owner = jax.vmap(lambda own, number: shared_out(jax.random.fold_in(streams_of[2], 2), own, number, PAIR_DEV, N_STA, 1, CAP, 2))(pair_owner_keys, pair_owner_turns).reshape((PAIRS, 1))
    pair_row = touch_ends(jax.random.randint(streams_of[3], (PAIRS,), 0, STA_DEV), jax.random.fold_in(streams_of[3], 1), 0, STA_DEV - 1).astype(jnp.int32)
    return {"spectra": spectra, "pair_source": pair_source, "pair_owner": pair_owner, "pair_row": pair_row}


two_pi = 2.0 * math.pi

def lag_table(start_bin, block_size, num_bins):
    bin_index = start_bin + jnp.arange(block_size, dtype=jnp.int32)
    lag_shift = jnp.arange(LAGS, dtype=jnp.int32) - LAGS // 2
    period = 2 * num_bins
    angles = jnp.mod(bin_index[:, None] * lag_shift[None, :], period).astype(jnp.float32) * (two_pi / period)
    return jnp.concatenate([jnp.cos(angles), -jnp.sin(angles)], axis=0).astype(jnp.bfloat16)

def cross_block(src_blk, rcv_blk):
    source_part = src_blk.astype(jnp.float32)
    recv_part = rcv_blk.astype(jnp.float32)
    src_re = source_part[..., 0:3, :][..., :, None, :]
    src_im = source_part[..., 3:6, :][..., :, None, :]
    rcv_re = recv_part[..., 0:3, :][..., None, :, :]
    rcv_im = recv_part[..., 3:6, :][..., None, :, :]
    cross_re = src_re * rcv_re + src_im * rcv_im
    cross_im = src_re * rcv_im - src_im * rcv_re
    return jnp.concatenate([cross_re, cross_im], axis=-1).astype(jnp.bfloat16)

def window_taper():
    lag_pos = jnp.arange(LAGS, dtype=jnp.float32)
    return 0.75 - 0.25 * jnp.cos(two_pi * (lag_pos + 0.5) / LAGS)

def reference(spectra, pair_source, pair_owner, pair_row):
    pair_index = jnp.arange(PAIRS, dtype=jnp.int32)
    src_station = (pair_index // (PAIR_DEV * N_GRP) * STA_DEV + pair_source).astype(jnp.int32)
    rcv_station = (pair_owner[:, 0] * STA_DEV + pair_row).astype(jnp.int32)
    group_size = math.gcd(PAIRS, 128)
    block_size = min(512, BINS)

    def one_group(ids):
        src_ids, rcv_ids = ids
        src_spec = jnp.take(spectra, src_ids, axis=1)
        rcv_spec = jnp.take(spectra, rcv_ids, axis=1)

        def add_block(block_index, running):
            start_bin = (block_index * block_size).astype(jnp.int32)
            src_blk = lax.dynamic_slice_in_dim(src_spec, start_bin, block_size, 3)
            rcv_blk = lax.dynamic_slice_in_dim(rcv_spec, start_bin, block_size, 3)
            cross = lax.optimization_barrier(cross_block(src_blk, rcv_blk))
            summed = lax.optimization_barrier(jnp.sum(cross.astype(jnp.float32), axis=0)).reshape(group_size * 9, 2 * block_size)
            table = lax.optimization_barrier(lag_table(start_bin, block_size, BINS)).astype(jnp.float32)
            return running + jnp.dot(summed, table, precision=lax.Precision.HIGHEST)
        running = lax.fori_loop(0, BINS // block_size, add_block, jnp.zeros((group_size * 9, LAGS), jnp.float32))
        return running.reshape(group_size, 9, LAGS)
    corr = lax.map(one_group, (src_station.reshape(-1, group_size), rcv_station.reshape(-1, group_size)))
    corr = corr.reshape(PAIRS, 9, LAGS)
    return corr * window_taper()[None, None, :] / (HOURS * math.sqrt(BINS))
```

```python
import math

import jax
import jax.numpy as jnp
from jax import lax
from jax.experimental import pallas as pl
from jax.experimental.pallas import tpu as pltpu
from jax.sharding import PartitionSpec as P

LAGS = 1024
NZ, NG, NY, NC, NX = 16, 8, 4, 2, 4
SD, PD, NB = 8, 16, 8192
W = NB // NG
WA = 512
FINE = 32
ROWS = NG * PD
CH = 128
TWO_PI = 2.0 * math.pi


def phases(bins):
    lag = jnp.arange(LAGS, dtype=jnp.int32) - LAGS // 2
    ang = jnp.mod(bins[:, None] * lag[None, :], 2 * NB).astype(jnp.float32) * (TWO_PI / (2 * NB))
    return jnp.cos(ang), jnp.sin(ang)


def correlate(ridx_ref, sidx_ref, xa_ref, xb_ref, hc_ref, hs_ref, lc_ref, ls_ref, keep_ref, send_ref, cross, table):
    lc, ls = lc_ref[...], ls_ref[...]

    def fill(i, carry):
        hc, hs = hc_ref[pl.ds(i, 1), :], hs_ref[pl.ds(i, 1), :]
        row = pl.multiple_of(i * FINE, FINE)
        table[pl.ds(row, FINE), :] = (hc * lc - hs * ls).astype(jnp.bfloat16)
        table[pl.ds(W + row, FINE), :] = (-(hs * lc + hc * ls)).astype(jnp.bfloat16)
        return carry

    lax.fori_loop(0, W // FINE, fill, 0)

    station = lax.broadcasted_iota(jnp.int32, (ROWS, NZ * SD), 1)
    pick_r = (station == ridx_ref[...]).astype(jnp.float32).astype(jnp.bfloat16)
    pick_s = (station == sidx_ref[...]).astype(jnp.float32).astype(jnp.bfloat16)
    for k in range(W // CH):
        at = k * CH
        ref, lo = (xa_ref, at) if at < WA else (xb_ref, at - WA)
        rcv, src = [], []
        for comp in range(6):
            x = ref[:, comp, :, lo : lo + CH].astype(jnp.float32).reshape(NZ * SD, CH).astype(jnp.bfloat16)
            rcv.append(jnp.dot(pick_r, x, preferred_element_type=jnp.float32))
            src.append(jnp.dot(pick_s, x, preferred_element_type=jnp.float32))
        for a in range(3):
            for b in range(3):
                r0 = (3 * a + b) * ROWS
                re = src[a] * rcv[b] + src[3 + a] * rcv[3 + b]
                im = src[a] * rcv[3 + b] - src[3 + a] * rcv[b]
                cross[r0 : r0 + ROWS, at : at + CH] = re.astype(jnp.bfloat16)
                cross[r0 : r0 + ROWS, W + at : W + at + CH] = im.astype(jnp.bfloat16)

    half = ROWS // 2
    for n in range(0, LAGS, 256):
        for a in range(3):
            out = jnp.dot(
                cross[a * 3 * ROWS : (a + 1) * 3 * ROWS, :], table[:, n : n + 256], preferred_element_type=jnp.float32
            )
            for b in range(3):
                for k in range(NY):
                    r0 = b * ROWS + k * PD
                    keep_ref[k, 3 * a + b, :, n : n + 256] = out[r0 : r0 + PD]
                    send_ref[k, 3 * a + b, :, n : n + 256] = out[half + r0 : half + r0 + PD].astype(jnp.bfloat16)


def body(spectra, pair_source, pair_owner, pair_row):
    s, g = lax.axis_index("sta"), lax.axis_index("grp")
    y, core = g // NC, g % NC

    code = (pair_owner[:, 0] * SD + pair_row) * (NZ * SD) + s * SD + pair_source
    code = lax.all_to_all(jnp.broadcast_to(code[None], (NG, PD)), "grp", 0, 0, tiled=True).reshape(NY, NC, PD)

    mine = lax.dynamic_slice_in_dim(spectra[0], g * W, W, 2).transpose(1, 0, 2)
    xa = lax.all_gather(mine[:, :, :WA], "sta", axis=0)
    xb = lax.all_gather(mine[:, :, WA:], "sta", axis=0)

    code = lax.dynamic_slice_in_dim(jnp.concatenate([code, code], axis=0), y, NY, 0)
    code = jnp.where(core == 0, code, code[:, ::-1]).transpose(1, 0, 2).reshape(ROWS, 1)
    hc, hs = phases(g * W + FINE * jnp.arange(W // FINE, dtype=jnp.int32))
    lc, ls = phases(jnp.arange(FINE, dtype=jnp.int32))
    shape = (NY, 9, PD, LAGS)
    keep, send = pl.pallas_call(
        correlate,
        out_shape=(jax.ShapeDtypeStruct(shape, jnp.float32), jax.ShapeDtypeStruct(shape, jnp.bfloat16)),
        in_specs=[pl.BlockSpec(memory_space=pltpu.VMEM)] * 8,
        out_specs=(pl.BlockSpec(memory_space=pltpu.VMEM),) * 2,
        scratch_shapes=[pltpu.VMEM((9 * ROWS, 2 * W), jnp.bfloat16), pltpu.VMEM((2 * W, LAGS), jnp.bfloat16)],
        compiler_params=pltpu.CompilerParams(vmem_limit_bytes=48 * 1024 * 1024),
        name="correlate",
    )(code // (NZ * SD), code % (NZ * SD), xa, xb, hc, hs, lc, ls)

    part = keep + lax.ppermute(send, "grp", [(i, i ^ 1) for i in range(NG)]).astype(jnp.float32)
    total = part[0]
    for k in range(1, NY):
        perm = [(i, (i + NC * k) % NG) for i in range(NG)]
        total = total + lax.ppermute(part[k].astype(jnp.bfloat16), "grp", perm).astype(jnp.float32)
    hours = jnp.broadcast_to(total.astype(jnp.bfloat16)[None], (NX, 9, PD, LAGS))
    hours = lax.all_to_all(hours, "hr", 0, 0, tiled=True).astype(jnp.float32)
    stacked = (hours[0] + hours[1] + (hours[2] + hours[3])).transpose(1, 0, 2)
    pos = jnp.arange(LAGS, dtype=jnp.float32)
    taper = 0.75 - 0.25 * jnp.cos(TWO_PI * (pos + 0.5) / LAGS)
    return stacked * (taper / (NX * math.sqrt(NB)))[None, None, :]


def solution(mesh):
    placed = (
        P("hr", "sta", None, None),
        P(("sta", "grp")),
        P(("sta", "grp"), None),
        P(("sta", "grp")),
    )
    return jax.shard_map(
        body, mesh=mesh, in_specs=placed, out_specs=P(("sta", "grp"), None, None), check_vma=False
    )
```

```python
import math

import jax
import jax.numpy as jnp
from jax import lax
from jax.experimental import pallas as pl
from jax.experimental.pallas import tpu as pltpu
from jax.sharding import PartitionSpec as P

LAGS = 1024
NZ, NG, NY, NC, NX = 16, 8, 4, 2, 4
SD, PD, NB = 8, 16, 8192
W = NB // NG
FINE = 32
ROWS = NG * PD
CH = 128
TW = LAGS // NX
TWO_PI = 2.0 * math.pi
VMEM_LIMIT = 48 * 1024 * 1024


def phases(bins):
    lag = jnp.arange(LAGS, dtype=jnp.int32) - LAGS // 2
    ang = jnp.mod(bins[:, None] * lag[None, :], 2 * NB).astype(jnp.float32) * (TWO_PI / (2 * NB))
    return jnp.cos(ang), jnp.sin(ang)


def one_hot(index, count):
    column = lax.broadcasted_iota(jnp.int32, (ROWS, count), 1)
    return (column == index).astype(jnp.float32).astype(jnp.bfloat16)


def prepare(sidx_ref, mine_ref, hc_ref, hs_ref, lc_ref, ls_ref, table, src):
    lc, ls = lc_ref[...], ls_ref[...]

    def fill(i, carry):
        hc, hs = hc_ref[pl.ds(i, 1), :], hs_ref[pl.ds(i, 1), :]
        row = pl.multiple_of(i * FINE, FINE)
        table[pl.ds(row, FINE), :] = (hc * lc - hs * ls).astype(jnp.bfloat16)
        table[pl.ds(W + row, FINE), :] = (-(hs * lc + hc * ls)).astype(jnp.bfloat16)
        return carry

    lax.fori_loop(0, W // FINE, fill, 0)
    pick = one_hot(sidx_ref[...], SD)
    for comp in range(6):
        src[comp] = jnp.dot(pick, mine_ref[comp], preferred_element_type=jnp.float32).astype(jnp.bfloat16)


def correlate(ridx_ref, near_ref, left_ref, right_ref, table, src, keep_ref, send_ref, cross):
    pick = one_hot(ridx_ref[...], NZ * SD)
    for k in range(W // CH):
        at = k * CH
        rcv = []
        for comp in range(6):
            x = [
                ref[:, comp, :, at : at + CH].astype(jnp.float32).reshape(-1, CH)
                for ref in (near_ref, left_ref, right_ref)
            ]
            x = jnp.concatenate(x, axis=0).astype(jnp.bfloat16)
            rcv.append(jnp.dot(pick, x, preferred_element_type=jnp.float32))
        s = [src[comp, :, at : at + CH].astype(jnp.float32) for comp in range(6)]
        for a in range(3):
            for b in range(3):
                r0 = (3 * a + b) * ROWS
                re = s[a] * rcv[b] + s[3 + a] * rcv[3 + b]
                im = s[a] * rcv[3 + b] - s[3 + a] * rcv[b]
                cross[r0 : r0 + ROWS, at : at + CH] = re.astype(jnp.bfloat16)
                cross[r0 : r0 + ROWS, W + at : W + at + CH] = im.astype(jnp.bfloat16)

    half = ROWS // 2
    for n in range(NX):
        for a in range(3):
            out = jnp.dot(
                cross[a * 3 * ROWS : (a + 1) * 3 * ROWS, :],
                table[:, n * TW : (n + 1) * TW],
                preferred_element_type=jnp.float32,
            )
            for b in range(3):
                for k in range(NY):
                    r0 = b * ROWS + k * PD
                    keep_ref[k, n, 3 * a + b] = out[r0 : r0 + PD]
                    send_ref[k, n, 3 * a + b] = out[half + r0 : half + r0 + PD].astype(jnp.bfloat16)


def vmem(n):
    return [pl.BlockSpec(memory_space=pltpu.VMEM)] * n


def body(spectra, pair_source, pair_owner, pair_row):
    s, g = lax.axis_index("sta"), lax.axis_index("grp")
    core, parity = g % NC, s % 2

    mine = lax.dynamic_slice_in_dim(spectra[0], g * W, W, 2).transpose(1, 0, 2)
    planes = [list(range(p, NZ, 2)) for p in range(2)]
    near = lax.all_gather(mine, "sta", axis=0, axis_index_groups=planes)
    left = lax.ppermute(near[: NZ // 4], "sta", [(i, (i + 1) % NZ) for i in range(NZ)])
    right = lax.ppermute(near[NZ // 4 :], "sta", [(i, (i - 1) % NZ) for i in range(NZ)])

    owner = pair_owner[:, 0]
    slot = jnp.where(owner % 2 == parity, 0, NZ // 2) + owner // 2
    code = (slot * SD + pair_row) * SD + pair_source
    code = jnp.broadcast_to(code[None], (NG, PD))
    code, near = lax.optimization_barrier((code, near))
    code = lax.all_to_all(code, "grp", 0, 0, tiled=True).reshape(NY, NC, PD)
    code = jnp.where(core == 0, code, code[:, ::-1]).transpose(1, 0, 2).reshape(ROWS, 1)

    hc, hs = phases(g * W + FINE * jnp.arange(W // FINE, dtype=jnp.int32))
    lc, ls = phases(jnp.arange(FINE, dtype=jnp.int32))
    params = pltpu.CompilerParams(vmem_limit_bytes=VMEM_LIMIT)
    table, src = pl.pallas_call(
        prepare,
        out_shape=(
            jax.ShapeDtypeStruct((2 * W, LAGS), jnp.bfloat16),
            jax.ShapeDtypeStruct((6, ROWS, W), jnp.bfloat16),
        ),
        in_specs=vmem(6),
        out_specs=tuple(vmem(2)),
        compiler_params=params,
        name="prepare",
    )(code % SD, mine, hc, hs, lc, ls)
    shape = (NY, NX, 9, PD, TW)
    keep, send = pl.pallas_call(
        correlate,
        out_shape=(jax.ShapeDtypeStruct(shape, jnp.float32), jax.ShapeDtypeStruct(shape, jnp.bfloat16)),
        in_specs=vmem(6),
        out_specs=tuple(vmem(2)),
        scratch_shapes=[pltpu.VMEM((9 * ROWS, 2 * W), jnp.bfloat16)],
        compiler_params=params,
        name="correlate",
    )(code // SD, near, left, right, table, src)

    part = keep + lax.ppermute(send, "grp", [(i, i ^ 1) for i in range(NG)]).astype(jnp.float32)
    part = part.astype(jnp.bfloat16).reshape(NY * NX, 9, PD, TW)
    chips = [[(NC * y + c) * NX + x for y in range(NY) for x in range(NX)] for c in range(NC)]
    part = lax.all_to_all(part, ("grp", "hr"), 0, 0, axis_index_groups=chips, tiled=True)
    total = jnp.sum(part.astype(jnp.float32), axis=0)
    pos = lax.axis_index("hr") * TW + jnp.arange(TW, dtype=jnp.int32)
    taper = 0.75 - 0.25 * jnp.cos(TWO_PI * (pos.astype(jnp.float32) + 0.5) / LAGS)
    total = total * (taper / (NX * math.sqrt(NB)))
    return lax.all_gather(total, "hr", axis=2, tiled=True).transpose(1, 0, 2)


def solution(mesh):
    placed = (
        P("hr", "sta", None, None),
        P(("sta", "grp")),
        P(("sta", "grp"), None),
        P(("sta", "grp")),
    )
    return jax.shard_map(
        body, mesh=mesh, in_specs=placed, out_specs=P(("sta", "grp"), None, None), check_vma=False
    )
```

```python
import functools
import math

import jax
import jax.numpy as jnp
from jax import lax
from jax.experimental import pallas as pl
from jax.experimental.pallas import tpu as pltpu
from jax.sharding import PartitionSpec as P

LAGS = 1024
NZ, NG, NY, NC, NX = 16, 8, 4, 2, 4
SD, PD, NB = 8, 16, 8192
W = NB // NG
FINE = 32
HALF = NY * PD
CH = 128
TW = LAGS // NX
TWO_PI = 2.0 * math.pi
VMEM_LIMIT = 24 * 1024 * 1024


def phases(bins):
    lag = jnp.arange(LAGS, dtype=jnp.int32) - LAGS // 2
    ang = jnp.mod(bins[:, None] * lag[None, :], 2 * NB).astype(jnp.float32) * (TWO_PI / (2 * NB))
    return jnp.cos(ang), jnp.sin(ang)


def one_hot(index, count):
    column = lax.broadcasted_iota(jnp.int32, (HALF, count), 1)
    return (column == index).astype(jnp.float32).astype(jnp.bfloat16)


def lag_table(hc_ref, hs_ref, lc_ref, ls_ref, table):
    lc, ls = lc_ref[...], ls_ref[...]

    def fill(i, carry):
        hc, hs = hc_ref[pl.ds(i, 1), :], hs_ref[pl.ds(i, 1), :]
        row = pl.multiple_of(i * FINE, FINE)
        table[pl.ds(row, FINE), :] = (hc * lc - hs * ls).astype(jnp.bfloat16)
        table[pl.ds(W + row, FINE), :] = (-(hs * lc + hc * ls)).astype(jnp.bfloat16)
        return carry

    lax.fori_loop(0, W // FINE, fill, 0)


def correlate(half, ridx_ref, sidx_ref, mine_ref, near_ref, left_ref, right_ref, table, out_ref, cross):
    pick_r = one_hot(ridx_ref[half * HALF : (half + 1) * HALF], NZ * SD)
    pick_s = one_hot(sidx_ref[half * HALF : (half + 1) * HALF], SD)
    for k in range(W // CH):
        at = k * CH
        r, s = [], []
        for comp in range(6):
            x = [
                ref[:, comp, :, at : at + CH].astype(jnp.float32).reshape(-1, CH)
                for ref in (near_ref, left_ref, right_ref)
            ]
            x = jnp.concatenate(x, axis=0).astype(jnp.bfloat16)
            r.append(jnp.dot(pick_r, x, preferred_element_type=jnp.float32))
            s.append(jnp.dot(pick_s, mine_ref[comp, :, at : at + CH], preferred_element_type=jnp.float32))
        for a in range(3):
            for b in range(3):
                r0 = (3 * a + b) * HALF
                re = s[a] * r[b] + s[3 + a] * r[3 + b]
                im = s[a] * r[3 + b] - s[3 + a] * r[b]
                cross[r0 : r0 + HALF, at : at + CH] = re.astype(jnp.bfloat16)
                cross[r0 : r0 + HALF, W + at : W + at + CH] = im.astype(jnp.bfloat16)

    for n in range(NX):
        out = jnp.dot(cross[...], table[:, n * TW : (n + 1) * TW], preferred_element_type=jnp.float32)
        for c in range(9):
            for k in range(NY):
                r0 = c * HALF + k * PD
                out_ref[k, n, c] = out[r0 : r0 + PD].astype(out_ref.dtype)


def correlate_first(ridx, sidx, mine, near, left, right, hc, hs, lc, ls, out_ref, table, cross):
    lag_table(hc, hs, lc, ls, table)
    correlate(0, ridx, sidx, mine, near, left, right, table, out_ref, cross)


def vmem(n):
    return [pl.BlockSpec(memory_space=pltpu.VMEM)] * n


def body(spectra, pair_source, pair_owner, pair_row):
    s, g = lax.axis_index("sta"), lax.axis_index("grp")
    core, parity = g % NC, s % 2

    slot = jnp.where(pair_owner[:, 0] % 2 == parity, 0, NZ // 2) + pair_owner[:, 0] // 2
    code = ((slot * SD + pair_row) * SD + pair_source) * NG
    code = code[None] + lax.broadcasted_iota(jnp.int32, (NG, PD), 0)
    code = lax.all_to_all(code, "grp", 0, 0, tiled=True).reshape(NY, NC, PD) // NG
    code = jnp.where(core == 0, code[:, ::-1], code).transpose(1, 0, 2).reshape(NC * HALF, 1)

    mine = lax.dynamic_slice_in_dim(spectra[0], g * W, W, 2).transpose(1, 0, 2)
    planes = [list(range(p, NZ, 2)) for p in range(2)]
    near = lax.all_gather(mine, "sta", axis=0, axis_index_groups=planes)
    left = lax.ppermute(near[: NZ // 4], "sta", [(i, (i + 1) % NZ) for i in range(NZ)])
    right = lax.ppermute(near[NZ // 4 :], "sta", [(i, (i - 1) % NZ) for i in range(NZ)])

    pos = lax.axis_index("hr") * TW + jnp.arange(TW, dtype=jnp.int32)
    taper = 0.75 - 0.25 * jnp.cos(TWO_PI * (pos.astype(jnp.float32) + 0.5) / LAGS)
    scale = taper / (NX * math.sqrt(NB))
    hc, hs = phases(g * W + FINE * jnp.arange(W // FINE, dtype=jnp.int32))
    lc, ls = phases(jnp.arange(FINE, dtype=jnp.int32))

    ridx, sidx = code // SD, code % SD
    ridx, sidx, scale = lax.optimization_barrier((ridx, sidx, scale))

    shape = (NY, NX, 9, PD, TW)
    scratch = [pltpu.VMEM((9 * HALF, 2 * W), jnp.bfloat16)]
    params = pltpu.CompilerParams(vmem_limit_bytes=VMEM_LIMIT)
    send, table = pl.pallas_call(
        correlate_first,
        out_shape=(jax.ShapeDtypeStruct(shape, jnp.bfloat16), jax.ShapeDtypeStruct((2 * W, LAGS), jnp.bfloat16)),
        in_specs=vmem(10),
        out_specs=tuple(vmem(2)),
        scratch_shapes=scratch,
        compiler_params=params,
        name="correlate_first",
    )(ridx, sidx, mine, near, left, right, hc, hs, lc, ls)
    keep = pl.pallas_call(
        functools.partial(correlate, 1),
        out_shape=jax.ShapeDtypeStruct(shape, jnp.float32),
        in_specs=vmem(7),
        out_specs=vmem(1)[0],
        scratch_shapes=scratch,
        compiler_params=params,
        name="correlate",
    )(ridx, sidx, mine, near, left, right, table)

    part = keep + lax.ppermute(send, "grp", [(i, i ^ 1) for i in range(NG)]).astype(jnp.float32)
    part = part.astype(jnp.bfloat16).reshape(NY * NX, 9, PD, TW)
    chips = [[(NC * y + c) * NX + x for y in range(NY) for x in range(NX)] for c in range(NC)]
    part = lax.all_to_all(part, ("grp", "hr"), 0, 0, axis_index_groups=chips, tiled=True)
    total = jnp.sum(part.astype(jnp.float32), axis=0)
    return lax.all_gather(total * scale, "hr", axis=2, tiled=True).transpose(1, 0, 2)


def solution(mesh):
    placed = (
        P("hr", "sta", None, None),
        P(("sta", "grp")),
        P(("sta", "grp"), None),
        P(("sta", "grp")),
    )
    return jax.shard_map(
        body, mesh=mesh, in_specs=placed, out_specs=P(("sta", "grp"), None, None), check_vma=False
    )
```

```python
import functools
import math

import jax
import jax.numpy as jnp
from jax import lax
from jax.experimental import pallas as pl
from jax.experimental.pallas import tpu as pltpu
from jax.sharding import PartitionSpec as P

LAGS = 1024
NZ, NG, NY, NC, NX = 16, 8, 4, 2, 4
SD, PD, NB = 8, 16, 8192
W = NB // NG
FINE = 32
HALF = NY * PD
CH = 128
TW = LAGS // NX
TWO_PI = 2.0 * math.pi
VMEM_LIMIT = 24 * 1024 * 1024


def phases(bins):
    lag = jnp.arange(LAGS, dtype=jnp.int32) - LAGS // 2
    ang = jnp.mod(bins[:, None] * lag[None, :], 2 * NB).astype(jnp.float32) * (TWO_PI / (2 * NB))
    return jnp.cos(ang), jnp.sin(ang)


def stage(hc_ref, hs_ref, lc_ref, ls_ref, near_ref, first_ref, second_ref, table, stations):
    lc, ls = lc_ref[...], ls_ref[...]

    def fill(i, carry):
        hc, hs = hc_ref[pl.ds(i, 1), :], hs_ref[pl.ds(i, 1), :]
        row = pl.multiple_of(i * FINE, FINE)
        table[pl.ds(row, FINE), :] = (hc * lc - hs * ls).astype(jnp.bfloat16)
        table[pl.ds(W + row, FINE), :] = (-(hs * lc + hc * ls)).astype(jnp.bfloat16)
        return carry

    lax.fori_loop(0, W // FINE, fill, 0)
    for comp in range(6):
        row = 0
        for ref in (near_ref, first_ref, second_ref):
            x = ref[:, comp].astype(jnp.float32).reshape(-1, W).astype(jnp.bfloat16)
            stations[comp, row : row + x.shape[0]] = x
            row += x.shape[0]


def correlate(other, code_ref, core_ref, mine_ref, stations, table, out_ref, pick_r, pick_s, cross):
    core = core_ref[0] ^ other
    lane = lax.broadcasted_iota(jnp.int32, (1, NZ * SD), 1)

    def mark(p, carry):
        code = code_ref[p // PD * NC + core, p % PD]
        pick_r[pl.ds(p, 1), :] = (lane == code // SD).astype(jnp.float32)
        pick_s[pl.ds(p, 1), :] = (lane == code % SD).astype(jnp.float32)
        return carry

    lax.fori_loop(0, HALF, mark, 0, unroll=8)
    of_r = pick_r[...].astype(jnp.bfloat16)
    of_s = pick_s[:, :SD].astype(jnp.bfloat16)
    for k in range(W // CH):
        at = k * CH
        r, s = [], []
        for comp in range(6):
            r.append(jnp.dot(of_r, stations[comp, :, at : at + CH], preferred_element_type=jnp.float32))
            s.append(jnp.dot(of_s, mine_ref[comp, :, at : at + CH], preferred_element_type=jnp.float32))
        for a in range(3):
            for b in range(3):
                r0 = (3 * a + b) * HALF
                re = s[a] * r[b] + s[3 + a] * r[3 + b]
                im = s[a] * r[3 + b] - s[3 + a] * r[b]
                cross[r0 : r0 + HALF, at : at + CH] = re.astype(jnp.bfloat16)
                cross[r0 : r0 + HALF, W + at : W + at + CH] = im.astype(jnp.bfloat16)

    for n in range(NX):
        out = jnp.dot(cross[...], table[:, n * TW : (n + 1) * TW], preferred_element_type=jnp.float32)
        for c in range(9):
            for k in range(NY):
                r0 = c * HALF + k * PD
                out_ref[k, n, c] = out[r0 : r0 + PD].astype(out_ref.dtype)


def vmem(n):
    return [pl.BlockSpec(memory_space=pltpu.VMEM)] * n


def body(spectra, pair_source, pair_owner, pair_row):
    s, g = lax.axis_index("sta"), lax.axis_index("grp")
    core, parity = g % NC, s % 2

    mine = lax.dynamic_slice_in_dim(spectra[0], g * W, W, 2).transpose(1, 0, 2)
    planes = [list(range(p, NZ, 2)) for p in range(2)]
    near = lax.all_gather(mine, "sta", axis=0, axis_index_groups=planes)

    def neighbour(x, step):
        turn = [step if i % NC == 0 else -step for i in range(NG)]
        perm = [(z * NG + i, (z + turn[i]) % NZ * NG + i) for z in range(NZ) for i in range(NG)]
        return lax.ppermute(x, ("sta", "grp"), perm)

    first = neighbour(near[: NZ // 4], 1)
    second = neighbour(near[NZ // 4 :], -1)

    slot = jnp.where(pair_owner[:, 0] % 2 == parity, 0, NZ // 2) + pair_owner[:, 0] // 2
    code = (slot * SD + pair_row) * SD + pair_source
    pos = lax.axis_index("hr") * TW + jnp.arange(TW, dtype=jnp.int32)
    taper = 0.75 - 0.25 * jnp.cos(TWO_PI * (pos.astype(jnp.float32) + 0.5) / LAGS)
    scale = taper / (NX * math.sqrt(NB))
    hc, hs = phases(g * W + FINE * jnp.arange(W // FINE, dtype=jnp.int32))
    lc, ls = phases(jnp.arange(FINE, dtype=jnp.int32))
    near, code, hc, scale = lax.optimization_barrier((near, code, hc, scale))
    code = lax.all_to_all(jnp.broadcast_to(code[None], (NG, PD)), "grp", 0, 0, tiled=True)
    code, first, second = lax.optimization_barrier((code, first, second))

    params = pltpu.CompilerParams(vmem_limit_bytes=VMEM_LIMIT)
    table, stations = pl.pallas_call(
        stage,
        out_shape=(
            jax.ShapeDtypeStruct((2 * W, LAGS), jnp.bfloat16),
            jax.ShapeDtypeStruct((6, NZ * SD, W), jnp.bfloat16),
        ),
        in_specs=vmem(7),
        out_specs=tuple(vmem(2)),
        compiler_params=params,
        name="stage",
    )(hc, hs, lc, ls, near, first, second)

    def lags(other, dtype):
        return pl.pallas_call(
            functools.partial(correlate, other),
            out_shape=jax.ShapeDtypeStruct((NY, NX, 9, PD, TW), dtype),
            in_specs=[pl.BlockSpec(memory_space=pltpu.SMEM)] * 2 + vmem(3),
            out_specs=vmem(1)[0],
            scratch_shapes=[
                pltpu.VMEM((HALF, NZ * SD), jnp.float32),
                pltpu.VMEM((HALF, NZ * SD), jnp.float32),
                pltpu.VMEM((9 * HALF, 2 * W), jnp.bfloat16),
            ],
            compiler_params=params,
            name="correlate",
        )(code, core[None], mine, stations, table)

    send = lags(1, jnp.bfloat16)
    keep = lags(0, jnp.float32)
    part = keep + lax.ppermute(send, "grp", [(i, i ^ 1) for i in range(NG)]).astype(jnp.float32)
    part = part.astype(jnp.bfloat16).reshape(NY * NX, 9, PD, TW)
    chips = [[(NC * y + c) * NX + x for y in range(NY) for x in range(NX)] for c in range(NC)]
    part = lax.all_to_all(part, ("grp", "hr"), 0, 0, axis_index_groups=chips, tiled=True)
    total = jnp.sum(part.astype(jnp.float32), axis=0)
    return lax.all_gather(total * scale, "hr", axis=2, tiled=True).transpose(1, 0, 2)


def solution(mesh):
    placed = (
        P("hr", "sta", None, None),
        P(("sta", "grp")),
        P(("sta", "grp"), None),
        P(("sta", "grp")),
    )
    return jax.shard_map(
        body, mesh=mesh, in_specs=placed, out_specs=P(("sta", "grp"), None, None), check_vma=False
    )
```

```python
import functools
import math

import jax
import jax.numpy as jnp
from jax import lax
from jax.experimental import pallas as pl
from jax.experimental.pallas import tpu as pltpu
from jax.sharding import PartitionSpec as P

LAGS = 1024
NZ, NG, NY, NC, NX = 16, 8, 4, 2, 4
SD, PD, NB = 8, 16, 8192
W = NB // NG
BITS = 10
FINE = 32
HALF = NY * PD
CH = 128
TW = LAGS // NX
TWO_PI = 2.0 * math.pi
VMEM_LIMIT = 24 * 1024 * 1024


def codes(plane_ref, source_ref, owner_ref, row_ref, out_ref):
    plane, owner = plane_ref[0], owner_ref[...]
    slot = jnp.where(owner % 2 == plane % 2, 0, NZ // 2) + owner // 2
    code = (slot * SD + row_ref[...]) * (NZ * SD) + plane // 2 * SD + source_ref[...]
    out_ref[...] = jnp.broadcast_to(code, (NG, PD))


def stage(grp_ref, code_ref, near_ref, first_ref, second_ref, table, stations, pick, row, hi_c, hi_s):
    core, g = grp_ref[0] % NC, grp_ref[0]
    bit = lax.broadcasted_iota(jnp.int32, (16, LAGS), 0)
    lag = lax.broadcasted_iota(jnp.int32, (16, LAGS), 1) - LAGS // 2
    bins = jnp.where(bit < BITS, jnp.left_shift(1, bit), g * W)
    ang = ((bins * lag) & (2 * NB - 1)).astype(jnp.float32) * (TWO_PI / (2 * NB))
    cos, sin = jnp.cos(ang), jnp.sin(ang)

    def turned(c, s, bits):
        at = lax.broadcasted_iota(jnp.int32, (FINE, LAGS), 0)
        for k, b in enumerate(bits):
            on = (jnp.right_shift(at, k) & 1) == 1
            kc, ks = jnp.where(on, cos[b : b + 1], 1.0), jnp.where(on, sin[b : b + 1], 0.0)
            c, s = c * kc - s * ks, s * kc + c * ks
        return c, s

    half_bits = BITS // 2
    lc, ls = turned(jnp.ones((FINE, LAGS), jnp.float32), jnp.zeros((FINE, LAGS), jnp.float32), range(half_bits))
    base = jnp.broadcast_to(cos[BITS : BITS + 1], (FINE, LAGS)), jnp.broadcast_to(sin[BITS : BITS + 1], (FINE, LAGS))
    hi_c[...], hi_s[...] = turned(*base, range(half_bits, BITS))

    def fill(i, carry):
        hc, hs = hi_c[pl.ds(i, 1), :], hi_s[pl.ds(i, 1), :]
        at = pl.multiple_of(i * FINE, FINE)
        table[pl.ds(at, FINE), :] = (hc * lc - hs * ls).astype(jnp.bfloat16)
        table[pl.ds(W + at, FINE), :] = (-(hs * lc + hc * ls)).astype(jnp.bfloat16)
        return carry

    lax.fori_loop(0, W // FINE, fill, 0)

    even = core == 0
    for k in range(NY):
        c0, c1 = code_ref[NC * k : NC * k + 1], code_ref[NC * k + 1 : NC * k + 2]
        for half, code in enumerate((jnp.where(even, c1, c0), jnp.where(even, c0, c1))):
            at = half * 2 * HALF + k * PD
            row[0:1, at : at + PD] = code // (NZ * SD)
            row[0:1, at + HALF : at + HALF + PD] = code % (NZ * SD)
    station = lax.broadcasted_iota(jnp.int32, (NZ * SD, 2 * HALF), 0)
    for half in range(NC):
        hot = (station == row[0:1, half * 2 * HALF : (half + 1) * 2 * HALF]).astype(jnp.float32)
        pick[half] = hot.T.astype(jnp.bfloat16)
    for comp in range(6):
        at = 0
        for ref in (near_ref, first_ref, second_ref):
            x = ref[:, comp].astype(jnp.float32).reshape(-1, W).astype(jnp.bfloat16)
            stations[comp, at : at + x.shape[0]] = x
            at += x.shape[0]


def correlate(half, pick, stations, table, out_ref, cross):
    for k in range(W // CH):
        at = k * CH
        r, s = [], []
        for comp in range(6):
            x = jnp.dot(pick[half], stations[comp, :, at : at + CH], preferred_element_type=jnp.float32)
            r.append(x[:HALF])
            s.append(x[HALF:])
        for a in range(3):
            for b in range(3):
                r0 = (3 * a + b) * HALF
                re = s[a] * r[b] + s[3 + a] * r[3 + b]
                im = s[a] * r[3 + b] - s[3 + a] * r[b]
                cross[r0 : r0 + HALF, at : at + CH] = re.astype(jnp.bfloat16)
                cross[r0 : r0 + HALF, W + at : W + at + CH] = im.astype(jnp.bfloat16)

    for n in range(NX):
        out = jnp.dot(cross[...], table[:, n * TW : (n + 1) * TW], preferred_element_type=jnp.float32)
        for c in range(9):
            for k in range(NY):
                r0 = c * HALF + k * PD
                out_ref[k, n, c] = out[r0 : r0 + PD].astype(out_ref.dtype)


def vmem(n):
    return [pl.BlockSpec(memory_space=pltpu.VMEM)] * n


def body(spectra, pair_source, pair_owner, pair_row):
    s, g = lax.axis_index("sta"), lax.axis_index("grp")
    mine = lax.dynamic_slice_in_dim(spectra[0], g * W, W, 2).transpose(1, 0, 2)
    planes = [list(range(p, NZ, 2)) for p in range(2)]
    near = lax.all_gather(mine, "sta", axis=0, axis_index_groups=planes)

    def neighbour(x, step):
        turn = [step if i % NC == 0 else -step for i in range(NG)]
        perm = [(z * NG + i, (z + turn[i]) % NZ * NG + i) for z in range(NZ) for i in range(NG)]
        return lax.ppermute(x, ("sta", "grp"), perm)

    pos = lax.axis_index("hr") * TW + jnp.arange(TW, dtype=jnp.int32)
    taper = 0.75 - 0.25 * jnp.cos(TWO_PI * (pos.astype(jnp.float32) + 0.5) / LAGS)
    scale = taper / (NX * math.sqrt(NB))
    low, high = near[: NZ // 4], near[NZ // 4 :]
    low, high, pair_row = lax.optimization_barrier((low, high, pair_row))
    first, second = neighbour(low, 1), neighbour(high, -1)

    smem = pl.BlockSpec(memory_space=pltpu.SMEM)
    code = pl.pallas_call(
        codes,
        out_shape=jax.ShapeDtypeStruct((NG, PD), jnp.int32),
        in_specs=[smem] + vmem(3),
        out_specs=vmem(1)[0],
        cost_estimate=pl.CostEstimate(flops=10**10, bytes_accessed=10**6, transcendentals=0),
        name="codes",
    )(s[None], pair_source[None], pair_owner.T, pair_row[None])
    code = lax.all_to_all(code, "grp", 0, 0, tiled=True)
    code, first, second, scale = lax.optimization_barrier((code, first, second, scale))

    params = pltpu.CompilerParams(vmem_limit_bytes=VMEM_LIMIT)
    table, stations, pick = pl.pallas_call(
        stage,
        out_shape=(
            jax.ShapeDtypeStruct((2 * W, LAGS), jnp.bfloat16),
            jax.ShapeDtypeStruct((6, NZ * SD, W), jnp.bfloat16),
            jax.ShapeDtypeStruct((NC, 2 * HALF, NZ * SD), jnp.bfloat16),
        ),
        in_specs=[smem] + vmem(4),
        out_specs=tuple(vmem(3)),
        scratch_shapes=[
            pltpu.VMEM((8, NC * 2 * HALF), jnp.int32),
            pltpu.VMEM((FINE, LAGS), jnp.float32),
            pltpu.VMEM((FINE, LAGS), jnp.float32),
        ],
        compiler_params=params,
        name="stage",
    )(g[None], code, near, first, second)

    def lags(half, dtype):
        return pl.pallas_call(
            functools.partial(correlate, half),
            out_shape=jax.ShapeDtypeStruct((NY, NX, 9, PD, TW), dtype),
            in_specs=vmem(3),
            out_specs=vmem(1)[0],
            scratch_shapes=[pltpu.VMEM((9 * HALF, 2 * W), jnp.bfloat16)],
            compiler_params=params,
            name="correlate",
        )(pick, stations, table)

    send = lags(0, jnp.bfloat16)
    keep = lags(1, jnp.float32)
    part = keep + lax.ppermute(send, "grp", [(i, i ^ 1) for i in range(NG)]).astype(jnp.float32)
    part = part.astype(jnp.bfloat16).reshape(NY * NX, 9, PD, TW)
    chips = [[(NC * y + c) * NX + x for y in range(NY) for x in range(NX)] for c in range(NC)]
    part = lax.all_to_all(part, ("grp", "hr"), 0, 0, axis_index_groups=chips, tiled=True)
    total = jnp.sum(part.astype(jnp.float32), axis=0)
    return lax.all_gather(total * scale, "hr", axis=2, tiled=True).transpose(1, 0, 2)


def solution(mesh):
    placed = (
        P("hr", "sta", None, None),
        P(("sta", "grp")),
        P(("sta", "grp"), None),
        P(("sta", "grp")),
    )
    return jax.shard_map(
        body, mesh=mesh, in_specs=placed, out_specs=P(("sta", "grp"), None, None), check_vma=False
    )
```

```python
import functools
import math

import jax
import jax.numpy as jnp
from jax import lax
from jax.experimental import pallas as pl
from jax.experimental.pallas import tpu as pltpu
from jax.sharding import PartitionSpec as P

LAGS = 1024
NZ, NG, NY, NC, NX = 16, 8, 4, 2, 4
SD, PD, NB = 8, 16, 8192
W = NB // NG
NR = 4
BITS = 10
FINE = 32
HALF = NY * PD
CH = 128
TW = LAGS // NX
TWO_PI = 2.0 * math.pi
VMEM_LIMIT = 24 * 1024 * 1024


def codes(plane_ref, source_ref, owner_ref, row_ref, out_ref):
    plane, owner = plane_ref[0], owner_ref[...]
    away = (owner - plane) & (NR - 1)
    first = jnp.where(away == 0, 0, jnp.where(away == 3, 1, jnp.where(away == 1, 2, 3)))
    slot = first * (NZ // NR) + owner // NR
    code = (slot * SD + row_ref[...]) * (NZ * SD) + plane // NR * SD + source_ref[...]
    out_ref[...] = jnp.broadcast_to(code, (NG, PD))


def stage(grp_ref, code_ref, near_ref, first_ref, second_ref, third_ref, fourth_ref, table, stations, pick, row, hi_c, hi_s):
    core, g = grp_ref[0] % NC, grp_ref[0]
    bit = lax.broadcasted_iota(jnp.int32, (16, LAGS), 0)
    lag = lax.broadcasted_iota(jnp.int32, (16, LAGS), 1) - LAGS // 2
    bins = jnp.where(bit < BITS, jnp.left_shift(1, bit), g * W)
    ang = ((bins * lag) & (2 * NB - 1)).astype(jnp.float32) * (TWO_PI / (2 * NB))
    cos, sin = jnp.cos(ang), jnp.sin(ang)

    def turned(c, s, bits):
        at = lax.broadcasted_iota(jnp.int32, (FINE, LAGS), 0)
        for k, b in enumerate(bits):
            on = (jnp.right_shift(at, k) & 1) == 1
            kc, ks = jnp.where(on, cos[b : b + 1], 1.0), jnp.where(on, sin[b : b + 1], 0.0)
            c, s = c * kc - s * ks, s * kc + c * ks
        return c, s

    half_bits = BITS // 2
    lc, ls = turned(jnp.ones((FINE, LAGS), jnp.float32), jnp.zeros((FINE, LAGS), jnp.float32), range(half_bits))
    base = jnp.broadcast_to(cos[BITS : BITS + 1], (FINE, LAGS)), jnp.broadcast_to(sin[BITS : BITS + 1], (FINE, LAGS))
    hi_c[...], hi_s[...] = turned(*base, range(half_bits, BITS))

    def fill(i, carry):
        hc, hs = hi_c[pl.ds(i, 1), :], hi_s[pl.ds(i, 1), :]
        at = pl.multiple_of(i * FINE, FINE)
        table[pl.ds(at, FINE), :] = (hc * lc - hs * ls).astype(jnp.bfloat16)
        table[pl.ds(W + at, FINE), :] = (-(hs * lc + hc * ls)).astype(jnp.bfloat16)
        return carry

    lax.fori_loop(0, W // FINE, fill, 0)

    even = core == 0
    for k in range(NY):
        c0, c1 = code_ref[NC * k : NC * k + 1], code_ref[NC * k + 1 : NC * k + 2]
        for half, code in enumerate((jnp.where(even, c1, c0), jnp.where(even, c0, c1))):
            at = half * 2 * HALF + k * PD
            row[0:1, at : at + PD] = code // (NZ * SD)
            row[0:1, at + HALF : at + HALF + PD] = code % (NZ * SD)
    station = lax.broadcasted_iota(jnp.int32, (NZ * SD, 2 * HALF), 0)
    for half in range(NC):
        hot = (station == row[0:1, half * 2 * HALF : (half + 1) * 2 * HALF]).astype(jnp.float32)
        pick[half] = hot.T.astype(jnp.bfloat16)
    part = NZ * SD // NR
    rows = (0, pl.multiple_of(part + core * part, part), pl.multiple_of(2 * part - core * part, part), 3 * part, 7 * part // 2)
    for at, ref in zip(rows, (near_ref, first_ref, second_ref, third_ref, fourth_ref)):
        for comp in range(6):
            x = ref[:, comp].astype(jnp.float32).reshape(-1, W).astype(jnp.bfloat16)
            stations[comp, pl.ds(at, x.shape[0]), :] = x


def correlate(half, pick, stations, table, out_ref, cross):
    for k in range(W // CH):
        at = k * CH
        r, s = [], []
        for comp in range(6):
            x = jnp.dot(pick[half], stations[comp, :, at : at + CH], preferred_element_type=jnp.float32)
            r.append(x[:HALF])
            s.append(x[HALF:])
        for a in range(3):
            for b in range(3):
                r0 = (3 * a + b) * HALF
                re = s[a] * r[b] + s[3 + a] * r[3 + b]
                im = s[a] * r[3 + b] - s[3 + a] * r[b]
                cross[r0 : r0 + HALF, at : at + CH] = re.astype(jnp.bfloat16)
                cross[r0 : r0 + HALF, W + at : W + at + CH] = im.astype(jnp.bfloat16)

    for n in range(NX):
        out = jnp.dot(cross[...], table[:, n * TW : (n + 1) * TW], preferred_element_type=jnp.float32)
        for c in range(9):
            for k in range(NY):
                r0 = c * HALF + k * PD
                out_ref[k, n, c] = out[r0 : r0 + PD].astype(out_ref.dtype)


def vmem(n):
    return [pl.BlockSpec(memory_space=pltpu.VMEM)] * n


def body(spectra, pair_source, pair_owner, pair_row):
    s, g = lax.axis_index("sta"), lax.axis_index("grp")
    mine = lax.dynamic_slice_in_dim(spectra[0], g * W, W, 2).transpose(1, 0, 2)
    planes = [list(range(p, NZ, NR)) for p in range(NR)]
    near = lax.all_gather(mine, "sta", axis=0, axis_index_groups=planes)

    def neighbour(x, step):
        turn = [step if i % NC == 0 else -step for i in range(NG)]
        perm = [(z * NG + i, (z + turn[i]) % NZ * NG + i) for z in range(NZ) for i in range(NG)]
        return lax.ppermute(x, ("sta", "grp"), perm)

    pos = lax.axis_index("hr") * TW + jnp.arange(TW, dtype=jnp.int32)
    taper = 0.75 - 0.25 * jnp.cos(TWO_PI * (pos.astype(jnp.float32) + 0.5) / LAGS)
    scale = taper / (NX * math.sqrt(NB))
    half = NZ // NR // 2
    low, high, pair_row = lax.optimization_barrier((near[:half], near[half:], pair_row))
    moved = (neighbour(near, 1), neighbour(near, -1), neighbour(low, 2), neighbour(high, -2))

    smem = pl.BlockSpec(memory_space=pltpu.SMEM)
    code = pl.pallas_call(
        codes,
        out_shape=jax.ShapeDtypeStruct((NG, PD), jnp.int32),
        in_specs=[smem] + vmem(3),
        out_specs=vmem(1)[0],
        cost_estimate=pl.CostEstimate(flops=10**10, bytes_accessed=10**6, transcendentals=0),
        name="codes",
    )(s[None], pair_source[None], pair_owner.T, pair_row[None])
    code = lax.all_to_all(code, "grp", 0, 0, tiled=True)
    code, moved, scale = lax.optimization_barrier((code, moved, scale))

    params = pltpu.CompilerParams(vmem_limit_bytes=VMEM_LIMIT)
    table, stations, pick = pl.pallas_call(
        stage,
        out_shape=(
            jax.ShapeDtypeStruct((2 * W, LAGS), jnp.bfloat16),
            jax.ShapeDtypeStruct((6, NZ * SD, W), jnp.bfloat16),
            jax.ShapeDtypeStruct((NC, 2 * HALF, NZ * SD), jnp.bfloat16),
        ),
        in_specs=[smem] + vmem(6),
        out_specs=tuple(vmem(3)),
        scratch_shapes=[
            pltpu.VMEM((8, NC * 2 * HALF), jnp.int32),
            pltpu.VMEM((FINE, LAGS), jnp.float32),
            pltpu.VMEM((FINE, LAGS), jnp.float32),
        ],
        compiler_params=params,
        name="stage",
    )(g[None], code, near, *moved)

    def lags(half, dtype):
        return pl.pallas_call(
            functools.partial(correlate, half),
            out_shape=jax.ShapeDtypeStruct((NY, NX, 9, PD, TW), dtype),
            in_specs=vmem(3),
            out_specs=vmem(1)[0],
            scratch_shapes=[pltpu.VMEM((9 * HALF, 2 * W), jnp.bfloat16)],
            compiler_params=params,
            name="correlate",
        )(pick, stations, table)

    send = lags(0, jnp.bfloat16)
    keep = lags(1, jnp.float32)
    part = keep + lax.ppermute(send, "grp", [(i, i ^ 1) for i in range(NG)]).astype(jnp.float32)
    part = part.astype(jnp.bfloat16).reshape(NY * NX, 9, PD, TW)
    chips = [[(NC * y + c) * NX + x for y in range(NY) for x in range(NX)] for c in range(NC)]
    part = lax.all_to_all(part, ("grp", "hr"), 0, 0, axis_index_groups=chips, tiled=True)
    total = jnp.sum(part.astype(jnp.float32), axis=0)
    total = lax.all_gather((total * scale).astype(jnp.bfloat16), "hr", axis=2, tiled=True)
    return total.astype(jnp.float32).transpose(1, 0, 2)


def solution(mesh):
    placed = (
        P("hr", "sta", None, None),
        P(("sta", "grp")),
        P(("sta", "grp"), None),
        P(("sta", "grp")),
    )
    return jax.shard_map(
        body, mesh=mesh, in_specs=placed, out_specs=P(("sta", "grp"), None, None), check_vma=False
    )
```

```python
import functools
import math

import jax
import jax.numpy as jnp
from jax import lax
from jax.experimental import pallas as pl
from jax.experimental.pallas import tpu as pltpu
from jax.sharding import PartitionSpec as P

LAGS = 1024
NZ, NG, NY, NC, NX = 16, 8, 4, 2, 4
SD, PD, NB = 8, 16, 8192
W = NB // NG
STEP = 4
ORDER = (0, 12, 4, 8, 15, 11, 3, 7, 1, 13, 5, 9, 14, 10, 2, 6)
BITS = 10
FINE = 32
HALF = NY * PD
CH = 128
TW = LAGS // NX
TWO_PI = 2.0 * math.pi
VMEM_LIMIT = 24 * 1024 * 1024


def codes(plane_ref, source_ref, owner_ref, row_ref, out_ref):
    away = (owner_ref[...] - plane_ref[0]) & (NZ - 1)
    code = (away * SD + row_ref[...]) * SD + source_ref[...]
    out_ref[...] = jnp.broadcast_to(code, (NG, PD))


def stage(grp_ref, code_ref, near_ref, first_ref, second_ref, third_ref, fourth_ref, table, stations, pick, row, hi_c, hi_s):
    core, g = grp_ref[0] % NC, grp_ref[0]
    bit = lax.broadcasted_iota(jnp.int32, (16, LAGS), 0)
    lag = lax.broadcasted_iota(jnp.int32, (16, LAGS), 1) - LAGS // 2
    bins = jnp.where(bit < BITS, jnp.left_shift(1, bit), g * W)
    ang = ((bins * lag) & (2 * NB - 1)).astype(jnp.float32) * (TWO_PI / (2 * NB))
    cos, sin = jnp.cos(ang), jnp.sin(ang)

    def turned(c, s, bits):
        at = lax.broadcasted_iota(jnp.int32, (FINE, LAGS), 0)
        for k, b in enumerate(bits):
            on = (jnp.right_shift(at, k) & 1) == 1
            kc, ks = jnp.where(on, cos[b : b + 1], 1.0), jnp.where(on, sin[b : b + 1], 0.0)
            c, s = c * kc - s * ks, s * kc + c * ks
        return c, s

    half_bits = BITS // 2
    lc, ls = turned(jnp.ones((FINE, LAGS), jnp.float32), jnp.zeros((FINE, LAGS), jnp.float32), range(half_bits))
    base = jnp.broadcast_to(cos[BITS : BITS + 1], (FINE, LAGS)), jnp.broadcast_to(sin[BITS : BITS + 1], (FINE, LAGS))
    hi_c[...], hi_s[...] = turned(*base, range(half_bits, BITS))

    def fill(i, carry):
        hc, hs = hi_c[pl.ds(i, 1), :], hi_s[pl.ds(i, 1), :]
        at = pl.multiple_of(i * FINE, FINE)
        table[pl.ds(at, FINE), :] = (hc * lc - hs * ls).astype(jnp.bfloat16)
        table[pl.ds(W + at, FINE), :] = (-(hs * lc + hc * ls)).astype(jnp.bfloat16)
        return carry

    lax.fori_loop(0, W // FINE, fill, 0)

    even = core == 0
    for k in range(NY):
        c0, c1 = code_ref[NC * k : NC * k + 1], code_ref[NC * k + 1 : NC * k + 2]
        for half, code in enumerate((jnp.where(even, c1, c0), jnp.where(even, c0, c1))):
            at = half * 2 * HALF + k * PD
            away, place = code // (SD * SD), jnp.zeros_like(code)
            away = jnp.where(even, away, -away & (NZ - 1))
            for p, d in enumerate(ORDER):
                place = jnp.where(away == d, p, place)
            row[0:1, at : at + PD] = place * SD + code // SD % SD
            row[0:1, at + HALF : at + HALF + PD] = code % SD
    station = lax.broadcasted_iota(jnp.int32, (NZ * SD, 2 * HALF), 0)
    for half in range(NC):
        hot = (station == row[0:1, half * 2 * HALF : (half + 1) * 2 * HALF]).astype(jnp.float32)
        pick[half] = hot.T.astype(jnp.bfloat16)
    at = 0
    for ref in (near_ref, first_ref, second_ref, third_ref, fourth_ref):
        for comp in range(6):
            x = ref[:, comp].astype(jnp.float32).reshape(-1, W).astype(jnp.bfloat16)
            stations[comp, at : at + x.shape[0]] = x
        at += x.shape[0]


def correlate(half, pick, stations, table, out_ref, cross):
    for k in range(W // CH):
        at = k * CH
        r, s = [], []
        for comp in range(6):
            x = jnp.dot(pick[half], stations[comp, :, at : at + CH], preferred_element_type=jnp.float32)
            r.append(x[:HALF])
            s.append(x[HALF:])
        for a in range(3):
            for b in range(3):
                r0 = (3 * a + b) * HALF
                re = s[a] * r[b] + s[3 + a] * r[3 + b]
                im = s[a] * r[3 + b] - s[3 + a] * r[b]
                cross[r0 : r0 + HALF, at : at + CH] = re.astype(jnp.bfloat16)
                cross[r0 : r0 + HALF, W + at : W + at + CH] = im.astype(jnp.bfloat16)

    for n in range(NX):
        out = jnp.dot(cross[...], table[:, n * TW : (n + 1) * TW], preferred_element_type=jnp.float32)
        for c in range(9):
            for k in range(NY):
                r0 = c * HALF + k * PD
                out_ref[k, n, c] = out[r0 : r0 + PD].astype(out_ref.dtype)


def vmem(n):
    return [pl.BlockSpec(memory_space=pltpu.VMEM)] * n


def body(spectra, pair_source, pair_owner, pair_row):
    s, g = lax.axis_index("sta"), lax.axis_index("grp")
    mine = lax.dynamic_slice_in_dim(spectra[0], g * W, W, 2).transpose(1, 0, 2)

    def neighbour(x, step):
        turn = [step if i % NC == 0 else -step for i in range(NG)]
        perm = [(z * NG + i, (z + turn[i]) % NZ * NG + i) for z in range(NZ) for i in range(NG)]
        return lax.ppermute(x, ("sta", "grp"), perm)

    pos = lax.axis_index("hr") * TW + jnp.arange(TW, dtype=jnp.int32)
    taper = 0.75 - 0.25 * jnp.cos(TWO_PI * (pos.astype(jnp.float32) + 0.5) / LAGS)
    scale = taper / (NX * math.sqrt(NB))
    back, ahead = neighbour(mine, STEP), neighbour(mine, -STEP)
    far = jnp.concatenate([neighbour(back[:3], STEP), neighbour(ahead[3:], -STEP)])
    near = jnp.stack([mine, back, ahead, far])
    moved = (
        neighbour(near, 1),
        neighbour(near, -1),
        neighbour(jnp.stack([mine, back]), 2),
        neighbour(jnp.stack([mine, ahead]), -2),
    )

    smem = pl.BlockSpec(memory_space=pltpu.SMEM)
    code = pl.pallas_call(
        codes,
        out_shape=jax.ShapeDtypeStruct((NG, PD), jnp.int32),
        in_specs=[smem] + vmem(3),
        out_specs=vmem(1)[0],
        cost_estimate=pl.CostEstimate(flops=10**10, bytes_accessed=10**6, transcendentals=0),
        name="codes",
    )(s[None], pair_source[None], pair_owner.T, pair_row[None])
    code = lax.all_to_all(code, "grp", 0, 0, tiled=True)
    code, moved, scale = lax.optimization_barrier((code, moved, scale))

    params = pltpu.CompilerParams(vmem_limit_bytes=VMEM_LIMIT)
    table, stations, pick = pl.pallas_call(
        stage,
        out_shape=(
            jax.ShapeDtypeStruct((2 * W, LAGS), jnp.bfloat16),
            jax.ShapeDtypeStruct((6, NZ * SD, W), jnp.bfloat16),
            jax.ShapeDtypeStruct((NC, 2 * HALF, NZ * SD), jnp.bfloat16),
        ),
        in_specs=[smem] + vmem(6),
        out_specs=tuple(vmem(3)),
        scratch_shapes=[
            pltpu.VMEM((8, NC * 2 * HALF), jnp.int32),
            pltpu.VMEM((FINE, LAGS), jnp.float32),
            pltpu.VMEM((FINE, LAGS), jnp.float32),
        ],
        compiler_params=params,
        name="stage",
    )(g[None], code, near, *moved)

    def lags(half, dtype):
        return pl.pallas_call(
            functools.partial(correlate, half),
            out_shape=jax.ShapeDtypeStruct((NY, NX, 9, PD, TW), dtype),
            in_specs=vmem(3),
            out_specs=vmem(1)[0],
            scratch_shapes=[pltpu.VMEM((9 * HALF, 2 * W), jnp.bfloat16)],
            compiler_params=params,
            name="correlate",
        )(pick, stations, table)

    send = lags(0, jnp.bfloat16)
    keep = lags(1, jnp.float32)
    part = keep + lax.ppermute(send, "grp", [(i, i ^ 1) for i in range(NG)]).astype(jnp.float32)
    part = part.astype(jnp.bfloat16).reshape(NY * NX, 9, PD, TW)
    chips = [[(NC * y + c) * NX + x for y in range(NY) for x in range(NX)] for c in range(NC)]
    part = lax.all_to_all(part, ("grp", "hr"), 0, 0, axis_index_groups=chips, tiled=True)
    total = jnp.sum(part.astype(jnp.float32), axis=0)
    total = lax.all_gather((total * scale).astype(jnp.bfloat16), "hr", axis=2, tiled=True)
    return total.astype(jnp.float32).transpose(1, 0, 2)


def solution(mesh):
    placed = (
        P("hr", "sta", None, None),
        P(("sta", "grp")),
        P(("sta", "grp"), None),
        P(("sta", "grp")),
    )
    return jax.shard_map(
        body, mesh=mesh, in_specs=placed, out_specs=P(("sta", "grp"), None, None), check_vma=False
    )
```

```python
import functools
import math

import jax
import jax.numpy as jnp
from jax import lax
from jax.experimental import pallas as pl
from jax.experimental.pallas import tpu as pltpu
from jax.sharding import PartitionSpec as P

LAGS = 1024
NZ, NG, NY, NC, NX = 16, 8, 4, 2, 4
SD, PD, NB = 8, 16, 8192
W = NB // NG
STEP = 4
ORDER = (0, 12, 4, 8, 15, 11, 3, 7, 1, 13, 5, 9, 14, 10, 2, 6)
BITS = 10
FINE = 32
HALF = NY * PD
CH = 128
TW = LAGS // NX
TWO_PI = 2.0 * math.pi
VMEM_LIMIT = 24 * 1024 * 1024


def codes(plane_ref, source_ref, owner_ref, row_ref, out_ref):
    away = (owner_ref[...] - plane_ref[0]) & (NZ - 1)
    code = (away * SD + row_ref[...]) * SD + source_ref[...]
    out_ref[...] = jnp.broadcast_to(code, (NG, PD))


def stack(refs, stations, at):
    for ref in refs:
        for comp in range(6):
            x = ref[:, comp].astype(jnp.float32).reshape(-1, W).astype(jnp.bfloat16)
            stations[comp, at : at + x.shape[0]] = x
        at += x.shape[0]


def stage_far(grp_ref, code_ref, third_ref, fourth_ref, stations, pick, row):
    even = grp_ref[0] % NC == 0
    for k in range(NY):
        c0, c1 = code_ref[NC * k : NC * k + 1], code_ref[NC * k + 1 : NC * k + 2]
        for half, code in enumerate((jnp.where(even, c1, c0), jnp.where(even, c0, c1))):
            at = half * 2 * HALF + k * PD
            away, place = code // (SD * SD), jnp.zeros_like(code)
            away = jnp.where(even, away, -away & (NZ - 1))
            for p, d in enumerate(ORDER):
                place = jnp.where(away == d, p, place)
            row[0:1, at : at + PD] = place * SD + code // SD % SD
            row[0:1, at + HALF : at + HALF + PD] = code % SD
    station = lax.broadcasted_iota(jnp.int32, (NZ * SD, 2 * HALF), 0)
    for half in range(NC):
        hot = (station == row[0:1, half * 2 * HALF : (half + 1) * 2 * HALF]).astype(jnp.float32)
        pick[half] = hot.T.astype(jnp.bfloat16)
    stack((third_ref, fourth_ref), stations, 0)


def stage(grp_ref, near_ref, first_ref, second_ref, far_ref, table, stations, hi_c, hi_s):
    g = grp_ref[0]
    bit = lax.broadcasted_iota(jnp.int32, (16, LAGS), 0)
    lag = lax.broadcasted_iota(jnp.int32, (16, LAGS), 1) - LAGS // 2
    bins = jnp.where(bit < BITS, jnp.left_shift(1, bit), g * W)
    ang = ((bins * lag) & (2 * NB - 1)).astype(jnp.float32) * (TWO_PI / (2 * NB))
    cos, sin = jnp.cos(ang), jnp.sin(ang)

    def turned(c, s, bits):
        at = lax.broadcasted_iota(jnp.int32, (FINE, LAGS), 0)
        for k, b in enumerate(bits):
            on = (jnp.right_shift(at, k) & 1) == 1
            kc, ks = jnp.where(on, cos[b : b + 1], 1.0), jnp.where(on, sin[b : b + 1], 0.0)
            c, s = c * kc - s * ks, s * kc + c * ks
        return c, s

    half_bits = BITS // 2
    lc, ls = turned(jnp.ones((FINE, LAGS), jnp.float32), jnp.zeros((FINE, LAGS), jnp.float32), range(half_bits))
    base = jnp.broadcast_to(cos[BITS : BITS + 1], (FINE, LAGS)), jnp.broadcast_to(sin[BITS : BITS + 1], (FINE, LAGS))
    hi_c[...], hi_s[...] = turned(*base, range(half_bits, BITS))

    def fill(i, carry):
        hc, hs = hi_c[pl.ds(i, 1), :], hi_s[pl.ds(i, 1), :]
        at = pl.multiple_of(i * FINE, FINE)
        table[pl.ds(at, FINE), :] = (hc * lc - hs * ls).astype(jnp.bfloat16)
        table[pl.ds(W + at, FINE), :] = (-(hs * lc + hc * ls)).astype(jnp.bfloat16)
        return carry

    lax.fori_loop(0, W // FINE, fill, 0)

    stack((near_ref, first_ref, second_ref), stations, 0)
    stations[:, 12 * SD :] = far_ref[...]


def correlate(half, pick, stations, table, out_ref, cross):
    for k in range(W // CH):
        at = k * CH
        r, s = [], []
        for comp in range(6):
            x = jnp.dot(pick[half], stations[comp, :, at : at + CH], preferred_element_type=jnp.float32)
            r.append(x[:HALF])
            s.append(x[HALF:])
        for a in range(3):
            for b in range(3):
                r0 = (3 * a + b) * HALF
                re = s[a] * r[b] + s[3 + a] * r[3 + b]
                im = s[a] * r[3 + b] - s[3 + a] * r[b]
                cross[r0 : r0 + HALF, at : at + CH] = re.astype(jnp.bfloat16)
                cross[r0 : r0 + HALF, W + at : W + at + CH] = im.astype(jnp.bfloat16)

    for n in range(NX):
        out = jnp.dot(cross[...], table[:, n * TW : (n + 1) * TW], preferred_element_type=jnp.float32)
        for c in range(9):
            for k in range(NY):
                r0 = c * HALF + k * PD
                out_ref[k, n, c] = out[r0 : r0 + PD].astype(out_ref.dtype)


def vmem(n):
    return [pl.BlockSpec(memory_space=pltpu.VMEM)] * n


def body(spectra, pair_source, pair_owner, pair_row):
    s, g = lax.axis_index("sta"), lax.axis_index("grp")
    mine = lax.dynamic_slice_in_dim(spectra[0], g * W, W, 2).transpose(1, 0, 2)

    def neighbour(x, step):
        turn = [step if i % NC == 0 else -step for i in range(NG)]
        perm = [(z * NG + i, (z + turn[i]) % NZ * NG + i) for z in range(NZ) for i in range(NG)]
        return lax.ppermute(x, ("sta", "grp"), perm)

    pos = lax.axis_index("hr") * TW + jnp.arange(TW, dtype=jnp.int32)
    taper = 0.75 - 0.25 * jnp.cos(TWO_PI * (pos.astype(jnp.float32) + 0.5) / LAGS)
    scale = taper / (NX * math.sqrt(NB))
    mine, pair_row = lax.optimization_barrier((mine, pair_row))
    back, ahead = neighbour(mine, STEP), neighbour(mine, -STEP)

    long = pl.CostEstimate(flops=10**10, bytes_accessed=10**6, transcendentals=0)
    smem = pl.BlockSpec(memory_space=pltpu.SMEM)
    code = pl.pallas_call(
        codes,
        out_shape=jax.ShapeDtypeStruct((NG, PD), jnp.int32),
        in_specs=[smem] + vmem(3),
        out_specs=vmem(1)[0],
        cost_estimate=long,
        name="codes",
    )(s[None], pair_source[None], pair_owner.T, pair_row[None])
    code = lax.all_to_all(code, "grp", 0, 0, tiled=True)

    code, back, ahead, scale = lax.optimization_barrier((code, back, ahead, scale))
    far = jnp.concatenate([neighbour(back[:3], STEP), neighbour(ahead[3:], -STEP)])
    near = jnp.stack([mine, back, ahead, far])
    moved = (
        neighbour(near, 1),
        neighbour(near, -1),
        neighbour(jnp.stack([mine, back]), 2),
        neighbour(jnp.stack([mine, ahead]), -2),
    )

    params = pltpu.CompilerParams(vmem_limit_bytes=VMEM_LIMIT)
    first, second, third, fourth = moved
    far, pick = pl.pallas_call(
        stage_far,
        out_shape=(
            jax.ShapeDtypeStruct((6, 4 * SD, W), jnp.bfloat16),
            jax.ShapeDtypeStruct((NC, 2 * HALF, NZ * SD), jnp.bfloat16),
        ),
        in_specs=[smem] + vmem(3),
        out_specs=tuple(vmem(2)),
        scratch_shapes=[pltpu.VMEM((8, NC * 2 * HALF), jnp.int32)],
        cost_estimate=long,
        compiler_params=params,
        name="stage_far",
    )(g[None], code, third, fourth)
    far, pick, first, second = lax.optimization_barrier((far, pick, first, second))
    table, stations = pl.pallas_call(
        stage,
        out_shape=(
            jax.ShapeDtypeStruct((2 * W, LAGS), jnp.bfloat16),
            jax.ShapeDtypeStruct((6, NZ * SD, W), jnp.bfloat16),
        ),
        in_specs=[smem] + vmem(4),
        out_specs=tuple(vmem(2)),
        scratch_shapes=[pltpu.VMEM((FINE, LAGS), jnp.float32)] * 2,
        compiler_params=params,
        name="stage",
    )(g[None], near, first, second, far)

    def lags(half, dtype):
        return pl.pallas_call(
            functools.partial(correlate, half),
            out_shape=jax.ShapeDtypeStruct((NY, NX, 9, PD, TW), dtype),
            in_specs=vmem(3),
            out_specs=vmem(1)[0],
            scratch_shapes=[pltpu.VMEM((9 * HALF, 2 * W), jnp.bfloat16)],
            compiler_params=params,
            name="correlate",
        )(pick, stations, table)

    send = lags(0, jnp.bfloat16)
    keep = lags(1, jnp.float32)
    part = keep + lax.ppermute(send, "grp", [(i, i ^ 1) for i in range(NG)]).astype(jnp.float32)
    part = part.astype(jnp.bfloat16).reshape(NY * NX, 9, PD, TW)
    chips = [[(NC * y + c) * NX + x for y in range(NY) for x in range(NX)] for c in range(NC)]
    part = lax.all_to_all(part, ("grp", "hr"), 0, 0, axis_index_groups=chips, tiled=True)
    total = jnp.sum(part.astype(jnp.float32), axis=0)
    total = lax.all_gather((total * scale).astype(jnp.bfloat16), "hr", axis=2, tiled=True)
    return total.astype(jnp.float32).transpose(1, 0, 2)


def solution(mesh):
    placed = (
        P("hr", "sta", None, None),
        P(("sta", "grp")),
        P(("sta", "grp"), None),
        P(("sta", "grp")),
    )
    return jax.shard_map(
        body, mesh=mesh, in_specs=placed, out_specs=P(("sta", "grp"), None, None), check_vma=False
    )
```

```python
import functools
import math

import jax
import jax.numpy as jnp
from jax import lax
from jax.experimental import pallas as pl
from jax.experimental.pallas import tpu as pltpu
from jax.sharding import PartitionSpec as P

LAGS = 1024
NZ, NG, NY, NC, NX = 16, 8, 4, 2, 4
SD, PD, NB = 8, 16, 8192
W = NB // NG
NR = 4
BITS = 10
FINE = 32
HALF = NY * PD
CH = 128
TN = LAGS // 2
TA = TN + CH
TW = LAGS // NX
TWO_PI = 2.0 * math.pi
VMEM_LIMIT = 24 * 1024 * 1024


def codes(plane_ref, source_ref, owner_ref, row_ref, out_ref):
    plane, owner = plane_ref[0], owner_ref[...]
    away = (owner - plane) & (NR - 1)
    first = jnp.where(away == 0, 0, jnp.where(away == 3, 1, jnp.where(away == 1, 2, 3)))
    slot = first * (NZ // NR) + owner // NR
    code = (slot * SD + row_ref[...]) * (NZ * SD) + plane // NR * SD + source_ref[...]
    out_ref[...] = jnp.broadcast_to(code, (NG, PD))


def stage(grp_ref, code_ref, near_ref, first_ref, second_ref, third_ref, fourth_ref, table, edge, stations, pick, row, hi_c, hi_s):
    core, g = grp_ref[0] % NC, grp_ref[0]
    bit = lax.broadcasted_iota(jnp.int32, (16, TA), 0)
    lag = jnp.minimum(lax.broadcasted_iota(jnp.int32, (16, TA), 1), TN)
    bins = jnp.where(bit < BITS, jnp.left_shift(1, bit), g * W)
    ang = ((bins * lag) & (2 * NB - 1)).astype(jnp.float32) * (TWO_PI / (2 * NB))
    cos, sin = jnp.cos(ang), jnp.sin(ang)

    def turned(c, s, bits):
        at = lax.broadcasted_iota(jnp.int32, (FINE, TA), 0)
        for k, b in enumerate(bits):
            on = (jnp.right_shift(at, k) & 1) == 1
            kc, ks = jnp.where(on, cos[b : b + 1], 1.0), jnp.where(on, sin[b : b + 1], 0.0)
            c, s = c * kc - s * ks, s * kc + c * ks
        return c, s

    half_bits = BITS // 2
    lc, ls = turned(jnp.ones((FINE, TA), jnp.float32), jnp.zeros((FINE, TA), jnp.float32), range(half_bits))
    base = jnp.broadcast_to(cos[BITS : BITS + 1], (FINE, TA)), jnp.broadcast_to(sin[BITS : BITS + 1], (FINE, TA))
    hi_c[...], hi_s[...] = turned(*base, range(half_bits, BITS))

    zero = lax.broadcasted_iota(jnp.int32, (FINE, CH), 1) == 0

    def fill(i, carry):
        hc, hs = hi_c[pl.ds(i, 1), :], hi_s[pl.ds(i, 1), :]
        at = pl.multiple_of(i * FINE, FINE)
        c, s = hc * lc - hs * ls, hs * lc + hc * ls
        table[pl.ds(at, FINE), :] = c[:, :TN].astype(jnp.bfloat16)
        table[pl.ds(W + at, FINE), :] = (-s[:, :TN]).astype(jnp.bfloat16)
        table[pl.ds(W + at, FINE), 0:CH] = jnp.where(zero, s[:, TN:], -s[:, :CH]).astype(jnp.bfloat16)
        edge[pl.ds(at, FINE), :] = jnp.where(zero, c[:, TN:], 0.0).astype(jnp.bfloat16)
        return carry

    lax.fori_loop(0, W // FINE, fill, 0)

    even = core == 0
    for k in range(NY):
        c0, c1 = code_ref[NC * k : NC * k + 1], code_ref[NC * k + 1 : NC * k + 2]
        for half, code in enumerate((jnp.where(even, c1, c0), jnp.where(even, c0, c1))):
            at = half * 2 * HALF + k * PD
            row[0:1, at : at + PD] = code // (NZ * SD)
            row[0:1, at + HALF : at + HALF + PD] = code % (NZ * SD)
    station = lax.broadcasted_iota(jnp.int32, (NZ * SD, 2 * HALF), 0)
    for half in range(NC):
        hot = (station == row[0:1, half * 2 * HALF : (half + 1) * 2 * HALF]).astype(jnp.float32)
        pick[half] = hot.T.astype(jnp.bfloat16)
    part = NZ * SD // NR
    rows = (0, pl.multiple_of(part + core * part, part), pl.multiple_of(2 * part - core * part, part), 3 * part, 7 * part // 2)
    for at, ref in zip(rows, (near_ref, first_ref, second_ref, third_ref, fourth_ref)):
        for comp in range(6):
            x = ref[:, comp].astype(jnp.float32).reshape(-1, W).astype(jnp.bfloat16)
            stations[comp, pl.ds(at, x.shape[0]), :] = x


def correlate(half, pick, stations, table, edge, out_ref, cross):
    for k in range(W // CH):
        at = k * CH
        r, s = [], []
        for comp in range(6):
            x = jnp.dot(pick[half], stations[comp, :, at : at + CH], preferred_element_type=jnp.float32)
            r.append(x[:HALF])
            s.append(x[HALF:])
        for a in range(3):
            for b in range(3):
                r0 = (3 * a + b) * HALF
                re = s[a] * r[b] + s[3 + a] * r[3 + b]
                im = s[a] * r[3 + b] - s[3 + a] * r[b]
                cross[r0 : r0 + HALF, at : at + CH] = re.astype(jnp.bfloat16)
                cross[r0 : r0 + HALF, W + at : W + at + CH] = im.astype(jnp.bfloat16)

    for n in range(NX):
        odd, at = n // 2 * W, n % 2 * TW
        part = cross[:, odd : odd + W]
        out = jnp.dot(part, table[odd : odd + W, at : at + TW], preferred_element_type=jnp.float32)
        if n == 2:
            low = out[:, :CH] + jnp.dot(cross[:, :W], edge[...], preferred_element_type=jnp.float32)
            out = jnp.concatenate([low, out[:, CH:]], axis=1)
        for c in range(9):
            for k in range(NY):
                r0 = c * HALF + k * PD
                out_ref[k, n, c] = out[r0 : r0 + PD].astype(out_ref.dtype)


def unfold(scale_ref, x_ref, out_ref):
    x = x_ref[...].reshape(9 * PD, LAGS)
    even, odd = x[:, :TN], x[:, TN:]
    turn = lax.broadcasted_iota(jnp.int32, (TN, TN), 0) + lax.broadcasted_iota(jnp.int32, (TN, TN), 1) == TN
    turn = turn.astype(jnp.float32).astype(jnp.bfloat16)
    back = jnp.dot(even, turn, preferred_element_type=jnp.float32) - jnp.dot(odd, turn, preferred_element_type=jnp.float32)
    even, odd = even.astype(jnp.float32), odd.astype(jnp.float32)
    zero = lax.broadcasted_iota(jnp.int32, (9 * PD, TN), 1) == 0
    back = jnp.where(zero, odd, back) * scale_ref[:, :TN]
    ahead = jnp.where(zero, even, even + odd) * scale_ref[:, TN:]
    out_ref[:, :, :TN] = back.reshape(9, PD, TN)
    out_ref[:, :, TN:] = ahead.reshape(9, PD, TN)


def vmem(n):
    return [pl.BlockSpec(memory_space=pltpu.VMEM)] * n


def body(spectra, pair_source, pair_owner, pair_row):
    s, g = lax.axis_index("sta"), lax.axis_index("grp")
    mine = lax.dynamic_slice_in_dim(spectra[0], g * W, W, 2).transpose(1, 0, 2)
    planes = [list(range(p, NZ, NR)) for p in range(NR)]
    near = lax.all_gather(mine, "sta", axis=0, axis_index_groups=planes)

    def neighbour(x, step):
        turn = [step if i % NC == 0 else -step for i in range(NG)]
        perm = [(z * NG + i, (z + turn[i]) % NZ * NG + i) for z in range(NZ) for i in range(NG)]
        return lax.ppermute(x, ("sta", "grp"), perm)

    pos = jnp.arange(LAGS, dtype=jnp.float32)[None]
    taper = 0.75 - 0.25 * jnp.cos(TWO_PI * (pos + 0.5) / LAGS)
    scale = taper / (NX * math.sqrt(NB))
    half = NZ // NR // 2
    low, high, pair_row = lax.optimization_barrier((near[:half], near[half:], pair_row))
    moved = (neighbour(near, 1), neighbour(near, -1), neighbour(low, 2), neighbour(high, -2))

    smem = pl.BlockSpec(memory_space=pltpu.SMEM)
    code = pl.pallas_call(
        codes,
        out_shape=jax.ShapeDtypeStruct((NG, PD), jnp.int32),
        in_specs=[smem] + vmem(3),
        out_specs=vmem(1)[0],
        cost_estimate=pl.CostEstimate(flops=10**10, bytes_accessed=10**6, transcendentals=0),
        name="codes",
    )(s[None], pair_source[None], pair_owner.T, pair_row[None])
    code = lax.all_to_all(code, "grp", 0, 0, tiled=True)
    code, moved, scale = lax.optimization_barrier((code, moved, scale))

    params = pltpu.CompilerParams(vmem_limit_bytes=VMEM_LIMIT)
    table, edge, stations, pick = pl.pallas_call(
        stage,
        out_shape=(
            jax.ShapeDtypeStruct((2 * W, TN), jnp.bfloat16),
            jax.ShapeDtypeStruct((W, CH), jnp.bfloat16),
            jax.ShapeDtypeStruct((6, NZ * SD, W), jnp.bfloat16),
            jax.ShapeDtypeStruct((NC, 2 * HALF, NZ * SD), jnp.bfloat16),
        ),
        in_specs=[smem] + vmem(6),
        out_specs=tuple(vmem(4)),
        scratch_shapes=[
            pltpu.VMEM((8, NC * 2 * HALF), jnp.int32),
            pltpu.VMEM((FINE, TA), jnp.float32),
            pltpu.VMEM((FINE, TA), jnp.float32),
        ],
        compiler_params=params,
        name="stage",
    )(g[None], code, near, *moved)

    def lags(half, dtype):
        return pl.pallas_call(
            functools.partial(correlate, half),
            out_shape=jax.ShapeDtypeStruct((NY, NX, 9, PD, TW), dtype),
            in_specs=vmem(4),
            out_specs=vmem(1)[0],
            scratch_shapes=[pltpu.VMEM((9 * HALF, 2 * W), jnp.bfloat16)],
            compiler_params=params,
            name="correlate",
        )(pick, stations, table, edge)

    send = lags(0, jnp.bfloat16)
    keep = lags(1, jnp.float32)
    part = keep + lax.ppermute(send, "grp", [(i, i ^ 1) for i in range(NG)]).astype(jnp.float32)
    part = part.astype(jnp.bfloat16).reshape(NY * NX, 9, PD, TW)
    chips = [[(NC * y + c) * NX + x for y in range(NY) for x in range(NX)] for c in range(NC)]
    part = lax.all_to_all(part, ("grp", "hr"), 0, 0, axis_index_groups=chips, tiled=True)
    total = jnp.sum(part.astype(jnp.float32), axis=0).astype(jnp.bfloat16)
    total = lax.all_gather(total, "hr", axis=2, tiled=True)
    return pl.pallas_call(
        unfold,
        out_shape=jax.ShapeDtypeStruct((9, PD, LAGS), jnp.float32),
        in_specs=vmem(2),
        out_specs=vmem(1)[0],
        compiler_params=params,
        name="unfold",
    )(scale, total).transpose(1, 0, 2)


def solution(mesh):
    placed = (
        P("hr", "sta", None, None),
        P(("sta", "grp")),
        P(("sta", "grp"), None),
        P(("sta", "grp")),
    )
    return jax.shard_map(
        body, mesh=mesh, in_specs=placed, out_specs=P(("sta", "grp"), None, None), check_vma=False
    )
```

```python
import functools
import math

import jax
import jax.numpy as jnp
from jax import lax
from jax.experimental import pallas as pl
from jax.experimental.pallas import tpu as pltpu
from jax.sharding import PartitionSpec as P

LAGS = 1024
NZ, NG, NY, NC, NX = 16, 8, 4, 2, 4
SD, PD, NB = 8, 16, 8192
W = NB // NG
NR = 4
BITS = 10
FINE = 32
HALF = NY * PD
CH = 128
TN = LAGS // 2
TA = TN + CH
TW = LAGS // NX
TWO_PI = 2.0 * math.pi
VMEM_LIMIT = 24 * 1024 * 1024


def codes(plane_ref, source_ref, owner_ref, row_ref, out_ref):
    plane, owner = plane_ref[0], owner_ref[...]
    away = (owner - plane) & (NR - 1)
    first = jnp.where(away == 0, 0, jnp.where(away == 3, 1, jnp.where(away == 1, 2, 3)))
    slot = first * (NZ // NR) + owner // NR
    code = (slot * SD + row_ref[...]) * (NZ * SD) + plane // NR * SD + source_ref[...]
    out_ref[...] = jnp.broadcast_to(code, (NG, PD))


def one_hots(grp_ref, code_ref, pick, row):
    even = grp_ref[0] % NC == 0
    for k in range(NY):
        c0, c1 = code_ref[NC * k : NC * k + 1], code_ref[NC * k + 1 : NC * k + 2]
        for half, code in enumerate((jnp.where(even, c1, c0), jnp.where(even, c0, c1))):
            at = half * 2 * HALF + k * PD
            row[0:1, at : at + PD] = code // (NZ * SD)
            row[0:1, at + HALF : at + HALF + PD] = code % (NZ * SD)
    station = lax.broadcasted_iota(jnp.int32, (NZ * SD, 2 * HALF), 0)
    for half in range(NC):
        hot = (station == row[0:1, half * 2 * HALF : (half + 1) * 2 * HALF]).astype(jnp.float32)
        pick[half] = hot.T.astype(jnp.bfloat16)


def stage(grp_ref, near_ref, first_ref, second_ref, third_ref, fourth_ref, table, edge, stations, hi_c, hi_s):
    core, g = grp_ref[0] % NC, grp_ref[0]
    bit = lax.broadcasted_iota(jnp.int32, (16, TA), 0)
    lag = jnp.minimum(lax.broadcasted_iota(jnp.int32, (16, TA), 1), TN)
    bins = jnp.where(bit < BITS, jnp.left_shift(1, bit), g * W)
    ang = ((bins * lag) & (2 * NB - 1)).astype(jnp.float32) * (TWO_PI / (2 * NB))
    cos, sin = jnp.cos(ang), jnp.sin(ang)

    def turned(c, s, bits):
        at = lax.broadcasted_iota(jnp.int32, (FINE, TA), 0)
        for k, b in enumerate(bits):
            on = (jnp.right_shift(at, k) & 1) == 1
            kc, ks = jnp.where(on, cos[b : b + 1], 1.0), jnp.where(on, sin[b : b + 1], 0.0)
            c, s = c * kc - s * ks, s * kc + c * ks
        return c, s

    half_bits = BITS // 2
    lc, ls = turned(jnp.ones((FINE, TA), jnp.float32), jnp.zeros((FINE, TA), jnp.float32), range(half_bits))
    base = jnp.broadcast_to(cos[BITS : BITS + 1], (FINE, TA)), jnp.broadcast_to(sin[BITS : BITS + 1], (FINE, TA))
    hi_c[...], hi_s[...] = turned(*base, range(half_bits, BITS))

    zero = lax.broadcasted_iota(jnp.int32, (FINE, CH), 1) == 0

    def fill(i, carry):
        hc, hs = hi_c[pl.ds(i, 1), :], hi_s[pl.ds(i, 1), :]
        at = pl.multiple_of(i * FINE, FINE)
        c, s = hc * lc - hs * ls, hs * lc + hc * ls
        table[pl.ds(at, FINE), :] = c[:, :TN].astype(jnp.bfloat16)
        table[pl.ds(W + at, FINE), :] = (-s[:, :TN]).astype(jnp.bfloat16)
        table[pl.ds(W + at, FINE), 0:CH] = jnp.where(zero, s[:, TN:], -s[:, :CH]).astype(jnp.bfloat16)
        edge[pl.ds(at, FINE), :] = jnp.where(zero, c[:, TN:], 0.0).astype(jnp.bfloat16)
        return carry

    lax.fori_loop(0, W // FINE, fill, 0)

    part = NZ * SD // NR
    rows = (0, pl.multiple_of(part + core * part, part), pl.multiple_of(2 * part - core * part, part), 3 * part, 7 * part // 2)
    for at, ref in zip(rows, (near_ref, first_ref, second_ref, third_ref, fourth_ref)):
        for comp in range(6):
            x = ref[:, comp].astype(jnp.float32).reshape(-1, W).astype(jnp.bfloat16)
            stations[comp, pl.ds(at, x.shape[0]), :] = x


def correlate(half, pick, stations, table, edge, out_ref, cross):
    for k in range(W // CH):
        at = k * CH
        r, s = [], []
        for comp in range(6):
            x = jnp.dot(pick[half], stations[comp, :, at : at + CH], preferred_element_type=jnp.float32)
            r.append(x[:HALF])
            s.append(x[HALF:])
        for a in range(3):
            for b in range(3):
                r0 = (3 * a + b) * HALF
                re = s[a] * r[b] + s[3 + a] * r[3 + b]
                im = s[a] * r[3 + b] - s[3 + a] * r[b]
                cross[r0 : r0 + HALF, at : at + CH] = re.astype(jnp.bfloat16)
                cross[r0 : r0 + HALF, W + at : W + at + CH] = im.astype(jnp.bfloat16)

    for n in range(NX):
        odd, at = n // 2 * W, n % 2 * TW
        part = cross[:, odd : odd + W]
        out = jnp.dot(part, table[odd : odd + W, at : at + TW], preferred_element_type=jnp.float32)
        if n == 2:
            low = out[:, :CH] + jnp.dot(cross[:, :W], edge[...], preferred_element_type=jnp.float32)
            out = jnp.concatenate([low, out[:, CH:]], axis=1)
        for c in range(9):
            for k in range(NY):
                r0 = c * HALF + k * PD
                out_ref[k, n, c] = out[r0 : r0 + PD].astype(out_ref.dtype)


def unfold(scale_ref, x_ref, out_ref):
    x = x_ref[...].reshape(9 * PD, LAGS)
    even, odd = x[:, :TN], x[:, TN:]
    turn = lax.broadcasted_iota(jnp.int32, (TN, TN), 0) + lax.broadcasted_iota(jnp.int32, (TN, TN), 1) == TN
    turn = turn.astype(jnp.float32).astype(jnp.bfloat16)
    back = jnp.dot(even, turn, preferred_element_type=jnp.float32) - jnp.dot(odd, turn, preferred_element_type=jnp.float32)
    even, odd = even.astype(jnp.float32), odd.astype(jnp.float32)
    zero = lax.broadcasted_iota(jnp.int32, (9 * PD, TN), 1) == 0
    back = jnp.where(zero, odd, back) * scale_ref[:, :TN]
    ahead = jnp.where(zero, even, even + odd) * scale_ref[:, TN:]
    out_ref[:, :, :TN] = back.reshape(9, PD, TN)
    out_ref[:, :, TN:] = ahead.reshape(9, PD, TN)


def vmem(n):
    return [pl.BlockSpec(memory_space=pltpu.VMEM)] * n


def body(spectra, pair_source, pair_owner, pair_row):
    s, g = lax.axis_index("sta"), lax.axis_index("grp")
    mine = lax.dynamic_slice_in_dim(spectra[0], g * W, W, 2).transpose(1, 0, 2)
    planes = [list(range(p, NZ, NR)) for p in range(NR)]
    near = lax.all_gather(mine, "sta", axis=0, axis_index_groups=planes)

    def neighbour(x, step):
        turn = [step if i % NC == 0 else -step for i in range(NG)]
        perm = [(z * NG + i, (z + turn[i]) % NZ * NG + i) for z in range(NZ) for i in range(NG)]
        return lax.ppermute(x, ("sta", "grp"), perm)

    pos = jnp.arange(LAGS, dtype=jnp.float32)[None]
    taper = 0.75 - 0.25 * jnp.cos(TWO_PI * (pos + 0.5) / LAGS)
    scale = taper / (NX * math.sqrt(NB))
    half = NZ // NR // 2
    low, high, pair_row = lax.optimization_barrier((near[:half], near[half:], pair_row))
    first, second, third = neighbour(near, 1), neighbour(near, -1), neighbour(low, 2)

    long = pl.CostEstimate(flops=10**10, bytes_accessed=10**6, transcendentals=0)
    smem = pl.BlockSpec(memory_space=pltpu.SMEM)
    code = pl.pallas_call(
        codes,
        out_shape=jax.ShapeDtypeStruct((NG, PD), jnp.int32),
        in_specs=[smem] + vmem(3),
        out_specs=vmem(1)[0],
        cost_estimate=long,
        name="codes",
    )(s[None], pair_source[None], pair_owner.T, pair_row[None])
    code, high = lax.optimization_barrier((code, high))
    code = lax.all_to_all(code, "grp", 0, 0, tiled=True)
    moved = (first, second, third, neighbour(high, -2))
    params = pltpu.CompilerParams(vmem_limit_bytes=VMEM_LIMIT)
    pick = pl.pallas_call(
        one_hots,
        out_shape=jax.ShapeDtypeStruct((NC, 2 * HALF, NZ * SD), jnp.bfloat16),
        in_specs=[smem] + vmem(1),
        out_specs=vmem(1)[0],
        scratch_shapes=[pltpu.VMEM((8, NC * 2 * HALF), jnp.int32)],
        cost_estimate=long,
        compiler_params=params,
        name="one_hots",
    )(g[None], code)
    pick, moved, scale = lax.optimization_barrier((pick, moved, scale))
    table, edge, stations = pl.pallas_call(
        stage,
        out_shape=(
            jax.ShapeDtypeStruct((2 * W, TN), jnp.bfloat16),
            jax.ShapeDtypeStruct((W, CH), jnp.bfloat16),
            jax.ShapeDtypeStruct((6, NZ * SD, W), jnp.bfloat16),
        ),
        in_specs=[smem] + vmem(5),
        out_specs=tuple(vmem(3)),
        scratch_shapes=[
            pltpu.VMEM((FINE, TA), jnp.float32),
            pltpu.VMEM((FINE, TA), jnp.float32),
        ],
        compiler_params=params,
        name="stage",
    )(g[None], near, *moved)

    def lags(half, dtype):
        return pl.pallas_call(
            functools.partial(correlate, half),
            out_shape=jax.ShapeDtypeStruct((NY, NX, 9, PD, TW), dtype),
            in_specs=vmem(4),
            out_specs=vmem(1)[0],
            scratch_shapes=[pltpu.VMEM((9 * HALF, 2 * W), jnp.bfloat16)],
            compiler_params=params,
            name="correlate",
        )(pick, stations, table, edge)

    send = lags(0, jnp.bfloat16)
    keep = lags(1, jnp.float32)
    part = keep + lax.ppermute(send, "grp", [(i, i ^ 1) for i in range(NG)]).astype(jnp.float32)
    part = part.astype(jnp.bfloat16).reshape(NY * NX, 9, PD, TW)
    chips = [[(NC * y + c) * NX + x for y in range(NY) for x in range(NX)] for c in range(NC)]
    part = lax.all_to_all(part, ("grp", "hr"), 0, 0, axis_index_groups=chips, tiled=True)
    total = jnp.sum(part.astype(jnp.float32), axis=0).astype(jnp.bfloat16)
    total = lax.all_gather(total, "hr", axis=2, tiled=True)
    return pl.pallas_call(
        unfold,
        out_shape=jax.ShapeDtypeStruct((9, PD, LAGS), jnp.float32),
        in_specs=vmem(2),
        out_specs=vmem(1)[0],
        compiler_params=params,
        name="unfold",
    )(scale, total).transpose(1, 0, 2)


def solution(mesh):
    placed = (
        P("hr", "sta", None, None),
        P(("sta", "grp")),
        P(("sta", "grp"), None),
        P(("sta", "grp")),
    )
    return jax.shard_map(
        body, mesh=mesh, in_specs=placed, out_specs=P(("sta", "grp"), None, None), check_vma=False
    )
```

```python
import functools
import math

import jax
import jax.numpy as jnp
from jax import lax
from jax.experimental import pallas as pl
from jax.experimental.pallas import tpu as pltpu
from jax.sharding import PartitionSpec as P

LAGS = 1024
NZ, NG, NY, NC, NX = 16, 8, 4, 2, 4
SD, PD, NB = 8, 16, 8192
W = NB // NG
NR = 4
BITS = 10
FINE = 32
HALF = NY * PD
CH = 128
TN = LAGS // 2
TA = TN + CH
TW = LAGS // NX
TWO_PI = 2.0 * math.pi
VMEM_LIMIT = 24 * 1024 * 1024


def codes(plane_ref, source_ref, owner_ref, row_ref, out_ref):
    plane, owner = plane_ref[0], owner_ref[...]
    away = (owner - plane) & (NR - 1)
    first = jnp.where(away == 0, 0, jnp.where(away == 3, 1, jnp.where(away == 1, 2, 3)))
    slot = first * (NZ // NR) + owner // NR
    code = (slot * SD + row_ref[...]) * (NZ * SD) + plane // NR * SD + source_ref[...]
    out_ref[...] = jnp.broadcast_to(code, (NG, PD))


def one_hots(grp_ref, code_ref, pick, row):
    even = grp_ref[0] % NC == 0
    for k in range(NY):
        c0, c1 = code_ref[NC * k : NC * k + 1], code_ref[NC * k + 1 : NC * k + 2]
        for half, code in enumerate((jnp.where(even, c1, c0), jnp.where(even, c0, c1))):
            at = half * 2 * HALF + k * PD
            row[0:1, at : at + PD] = code // (NZ * SD)
            row[0:1, at + HALF : at + HALF + PD] = code % (NZ * SD)
    station = lax.broadcasted_iota(jnp.int32, (NZ * SD, 2 * HALF), 0)
    for half in range(NC):
        hot = (station == row[0:1, half * 2 * HALF : (half + 1) * 2 * HALF]).astype(jnp.float32)
        pick[half] = hot.T.astype(jnp.bfloat16)


def stage(grp_ref, near_ref, first_ref, second_ref, third_ref, fourth_ref, table, edge, stations, hi_c, hi_s):
    core, g = grp_ref[0] % NC, grp_ref[0]
    bit = lax.broadcasted_iota(jnp.int32, (16, TA), 0)
    lag = jnp.minimum(lax.broadcasted_iota(jnp.int32, (16, TA), 1), TN)
    bins = jnp.where(bit < BITS, jnp.left_shift(1, bit), g * W)
    ang = ((bins * lag) & (2 * NB - 1)).astype(jnp.float32) * (TWO_PI / (2 * NB))
    cos, sin = jnp.cos(ang), jnp.sin(ang)

    def turned(c, s, bits):
        at = lax.broadcasted_iota(jnp.int32, (FINE, TA), 0)
        for k, b in enumerate(bits):
            on = (jnp.right_shift(at, k) & 1) == 1
            kc, ks = jnp.where(on, cos[b : b + 1], 1.0), jnp.where(on, sin[b : b + 1], 0.0)
            c, s = c * kc - s * ks, s * kc + c * ks
        return c, s

    half_bits = BITS // 2
    lc, ls = turned(jnp.ones((FINE, TA), jnp.float32), jnp.zeros((FINE, TA), jnp.float32), range(half_bits))
    base = jnp.broadcast_to(cos[BITS : BITS + 1], (FINE, TA)), jnp.broadcast_to(sin[BITS : BITS + 1], (FINE, TA))
    hi_c[...], hi_s[...] = turned(*base, range(half_bits, BITS))

    zero = lax.broadcasted_iota(jnp.int32, (FINE, CH), 1) == 0

    def fill(i, carry):
        hc, hs = hi_c[pl.ds(i, 1), :], hi_s[pl.ds(i, 1), :]
        at = pl.multiple_of(i * FINE, FINE)
        c, s = hc * lc - hs * ls, hs * lc + hc * ls
        table[pl.ds(at, FINE), :] = c[:, :TN].astype(jnp.bfloat16)
        table[pl.ds(W + at, FINE), :] = (-s[:, :TN]).astype(jnp.bfloat16)
        table[pl.ds(W + at, FINE), 0:CH] = jnp.where(zero, s[:, TN:], -s[:, :CH]).astype(jnp.bfloat16)
        edge[pl.ds(at, FINE), :] = jnp.where(zero, c[:, TN:], 0.0).astype(jnp.bfloat16)
        return carry

    lax.fori_loop(0, W // FINE, fill, 0)

    part = NZ * SD // NR
    rows = (0, pl.multiple_of(part + core * part, part), pl.multiple_of(2 * part - core * part, part), 3 * part, 7 * part // 2)
    for at, ref in zip(rows, (near_ref, first_ref, second_ref, third_ref, fourth_ref)):
        for comp in range(6):
            x = ref[:, comp].astype(jnp.float32).reshape(-1, W).astype(jnp.bfloat16)
            stations[comp, pl.ds(at, x.shape[0]), :] = x


def correlate(half, pick, stations, table, edge, out_ref, cross):
    for k in range(W // CH):
        at = k * CH
        r, s = [], []
        for comp in range(6):
            x = jnp.dot(pick[half], stations[comp, :, at : at + CH], preferred_element_type=jnp.float32)
            r.append(x[:HALF])
            s.append(x[HALF:])
        for a in range(3):
            for b in range(3):
                r0 = (3 * a + b) * HALF
                re = s[a] * r[b] + s[3 + a] * r[3 + b]
                im = s[a] * r[3 + b] - s[3 + a] * r[b]
                cross[r0 : r0 + HALF, at : at + CH] = re.astype(jnp.bfloat16)
                cross[r0 : r0 + HALF, W + at : W + at + CH] = im.astype(jnp.bfloat16)

    for n in range(NX):
        odd, at = n // 2 * W, n % 2 * TW
        part = cross[:, odd : odd + W]
        out = jnp.dot(part, table[odd : odd + W, at : at + TW], preferred_element_type=jnp.float32)
        if n == 2:
            low = out[:, :CH] + jnp.dot(cross[:, :W], edge[...], preferred_element_type=jnp.float32)
            out = jnp.concatenate([low, out[:, CH:]], axis=1)
        for c in range(9):
            for k in range(NY):
                r0 = c * HALF + k * PD
                out_ref[k, n, c] = out[r0 : r0 + PD].astype(out_ref.dtype)


def unfold(scale_ref, x_ref, out_ref):
    x = x_ref[...].reshape(9 * PD, LAGS)
    even, odd = x[:, :TN], x[:, TN:]
    turn = lax.broadcasted_iota(jnp.int32, (TN, TN), 0) + lax.broadcasted_iota(jnp.int32, (TN, TN), 1) == TN
    turn = turn.astype(jnp.float32).astype(jnp.bfloat16)
    back = jnp.dot(even, turn, preferred_element_type=jnp.float32) - jnp.dot(odd, turn, preferred_element_type=jnp.float32)
    even, odd = even.astype(jnp.float32), odd.astype(jnp.float32)
    zero = lax.broadcasted_iota(jnp.int32, (9 * PD, TN), 1) == 0
    back = jnp.where(zero, odd, back) * scale_ref[:, :TN]
    ahead = jnp.where(zero, even, even + odd) * scale_ref[:, TN:]
    out_ref[:, :, :TN] = back.reshape(9, PD, TN)
    out_ref[:, :, TN:] = ahead.reshape(9, PD, TN)


def vmem(n):
    return [pl.BlockSpec(memory_space=pltpu.VMEM)] * n


def body(spectra, pair_source, pair_owner, pair_row):
    s, g = lax.axis_index("sta"), lax.axis_index("grp")
    smem = pl.BlockSpec(memory_space=pltpu.SMEM)
    code = pl.pallas_call(
        codes,
        out_shape=jax.ShapeDtypeStruct((NG, PD), jnp.int32),
        in_specs=[smem] + vmem(3),
        out_specs=vmem(1)[0],
        name="codes",
    )(s[None], pair_source[None], pair_owner.T, pair_row[None])
    code = lax.all_to_all(code, "grp", 0, 0, tiled=True)

    mine = lax.dynamic_slice_in_dim(spectra[0], g * W, W, 2).transpose(1, 0, 2)
    planes = [list(range(p, NZ, NR)) for p in range(NR)]
    near = lax.all_gather(mine, "sta", axis=0, axis_index_groups=planes)
    near, code = lax.optimization_barrier((near, code))

    def neighbour(x, step):
        turn = [step if i % NC == 0 else -step for i in range(NG)]
        perm = [(z * NG + i, (z + turn[i]) % NZ * NG + i) for z in range(NZ) for i in range(NG)]
        return lax.ppermute(x, ("sta", "grp"), perm)

    pos = jnp.arange(LAGS, dtype=jnp.float32)[None]
    taper = 0.75 - 0.25 * jnp.cos(TWO_PI * (pos + 0.5) / LAGS)
    scale = taper / (NX * math.sqrt(NB))
    half = NZ // NR // 2
    moved = (neighbour(near, 1), neighbour(near, -1), neighbour(near[:half], 2), neighbour(near[half:], -2))

    params = pltpu.CompilerParams(vmem_limit_bytes=VMEM_LIMIT)
    pick = pl.pallas_call(
        one_hots,
        out_shape=jax.ShapeDtypeStruct((NC, 2 * HALF, NZ * SD), jnp.bfloat16),
        in_specs=[smem] + vmem(1),
        out_specs=vmem(1)[0],
        scratch_shapes=[pltpu.VMEM((8, NC * 2 * HALF), jnp.int32)],
        compiler_params=params,
        name="one_hots",
    )(g[None], code)
    pick, moved, scale = lax.optimization_barrier((pick, moved, scale))
    table, edge, stations = pl.pallas_call(
        stage,
        out_shape=(
            jax.ShapeDtypeStruct((2 * W, TN), jnp.bfloat16),
            jax.ShapeDtypeStruct((W, CH), jnp.bfloat16),
            jax.ShapeDtypeStruct((6, NZ * SD, W), jnp.bfloat16),
        ),
        in_specs=[smem] + vmem(5),
        out_specs=tuple(vmem(3)),
        scratch_shapes=[
            pltpu.VMEM((FINE, TA), jnp.float32),
            pltpu.VMEM((FINE, TA), jnp.float32),
        ],
        compiler_params=params,
        name="stage",
    )(g[None], near, *moved)

    def lags(half, dtype):
        return pl.pallas_call(
            functools.partial(correlate, half),
            out_shape=jax.ShapeDtypeStruct((NY, NX, 9, PD, TW), dtype),
            in_specs=vmem(4),
            out_specs=vmem(1)[0],
            scratch_shapes=[pltpu.VMEM((9 * HALF, 2 * W), jnp.bfloat16)],
            compiler_params=params,
            name="correlate",
        )(pick, stations, table, edge)

    send = lags(0, jnp.bfloat16)
    keep = lags(1, jnp.float32)
    part = keep + lax.ppermute(send, "grp", [(i, i ^ 1) for i in range(NG)]).astype(jnp.float32)
    part = part.astype(jnp.bfloat16).reshape(NY * NX, 9, PD, TW)
    chips = [[(NC * y + c) * NX + x for y in range(NY) for x in range(NX)] for c in range(NC)]
    part = lax.all_to_all(part, ("grp", "hr"), 0, 0, axis_index_groups=chips, tiled=True)
    total = jnp.sum(part.astype(jnp.float32), axis=0).astype(jnp.bfloat16)
    total = lax.all_gather(total, "hr", axis=2, tiled=True)
    return pl.pallas_call(
        unfold,
        out_shape=jax.ShapeDtypeStruct((9, PD, LAGS), jnp.float32),
        in_specs=vmem(2),
        out_specs=vmem(1)[0],
        compiler_params=params,
        name="unfold",
    )(scale, total).transpose(1, 0, 2)


def solution(mesh):
    placed = (
        P("hr", "sta", None, None),
        P(("sta", "grp")),
        P(("sta", "grp"), None),
        P(("sta", "grp")),
    )
    return jax.shard_map(
        body, mesh=mesh, in_specs=placed, out_specs=P(("sta", "grp"), None, None), check_vma=False
    )
```

```python
import functools
import math

import jax
import jax.numpy as jnp
from jax import lax
from jax.experimental import pallas as pl
from jax.experimental.pallas import tpu as pltpu
from jax.sharding import PartitionSpec as P

LAGS = 1024
NZ, NG, NY, NC, NX = 16, 8, 4, 2, 4
SD, PD, NB = 8, 16, 8192
W = NB // NG
NR = 4
BITS = 10
FINE = 32
HALF = NY * PD
CH = 128
PC = 256
TN = LAGS // 2
TA = TN + CH
TW = LAGS // NX
TWO_PI = 2.0 * math.pi
VMEM_LIMIT = 24 * 1024 * 1024


def codes(plane_ref, source_ref, owner_ref, row_ref, out_ref):
    plane, owner = plane_ref[0], owner_ref[...]
    away = (owner - plane) & (NR - 1)
    first = jnp.where(away == 0, 0, jnp.where(away == 3, 1, jnp.where(away == 1, 2, 3)))
    slot = first * (NZ // NR) + owner // NR
    code = (slot * SD + row_ref[...]) * (NZ * SD) + plane // NR * SD + source_ref[...]
    out_ref[...] = jnp.broadcast_to(code, (NG, PD))


def stage(grp_ref, code_ref, near_ref, first_ref, second_ref, third_ref, fourth_ref, table, edge, stations, pick, row, hi_c, hi_s):
    core, g = grp_ref[0] % NC, grp_ref[0]
    bit = lax.broadcasted_iota(jnp.int32, (16, TA), 0)
    lag = jnp.minimum(lax.broadcasted_iota(jnp.int32, (16, TA), 1), TN)
    bins = jnp.where(bit < BITS, jnp.left_shift(1, bit), g * W)
    ang = ((bins * lag) & (2 * NB - 1)).astype(jnp.float32) * (TWO_PI / (2 * NB))
    cos, sin = jnp.cos(ang), jnp.sin(ang)

    def turned(c, s, bits):
        at = lax.broadcasted_iota(jnp.int32, (FINE, TA), 0)
        for k, b in enumerate(bits):
            on = (jnp.right_shift(at, k) & 1) == 1
            kc, ks = jnp.where(on, cos[b : b + 1], 1.0), jnp.where(on, sin[b : b + 1], 0.0)
            c, s = c * kc - s * ks, s * kc + c * ks
        return c, s

    half_bits = BITS // 2
    lc, ls = turned(jnp.ones((FINE, TA), jnp.float32), jnp.zeros((FINE, TA), jnp.float32), range(half_bits))
    base = jnp.broadcast_to(cos[BITS : BITS + 1], (FINE, TA)), jnp.broadcast_to(sin[BITS : BITS + 1], (FINE, TA))
    hi_c[...], hi_s[...] = turned(*base, range(half_bits, BITS))

    zero = lax.broadcasted_iota(jnp.int32, (FINE, CH), 1) == 0

    def fill(i, carry):
        hc, hs = hi_c[pl.ds(i, 1), :], hi_s[pl.ds(i, 1), :]
        at = pl.multiple_of(i * FINE, FINE)
        c, s = hc * lc - hs * ls, hs * lc + hc * ls
        table[pl.ds(at, FINE), :] = c[:, :TN].astype(jnp.bfloat16)
        table[pl.ds(W + at, FINE), :] = (-s[:, :TN]).astype(jnp.bfloat16)
        table[pl.ds(W + at, FINE), 0:CH] = jnp.where(zero, s[:, TN:], -s[:, :CH]).astype(jnp.bfloat16)
        edge[pl.ds(at, FINE), :] = jnp.where(zero, c[:, TN:], 0.0).astype(jnp.bfloat16)
        return carry

    lax.fori_loop(0, W // FINE, fill, 0)

    even = core == 0
    for k in range(NY):
        c0, c1 = code_ref[NC * k : NC * k + 1], code_ref[NC * k + 1 : NC * k + 2]
        for half, code in enumerate((jnp.where(even, c1, c0), jnp.where(even, c0, c1))):
            at = half * 2 * HALF + k * PD
            row[0:1, at : at + PD] = code // (NZ * SD)
            row[0:1, at + HALF : at + HALF + PD] = code % (NZ * SD)
    station = lax.broadcasted_iota(jnp.int32, (NZ * SD, 2 * HALF), 0)
    for half in range(NC):
        hot = (station == row[0:1, half * 2 * HALF : (half + 1) * 2 * HALF]).astype(jnp.float32)
        pick[half] = hot.T.astype(jnp.bfloat16)
    part = NZ * SD // NR
    rows = (0, pl.multiple_of(part + core * part, part), pl.multiple_of(2 * part - core * part, part), 3 * part, 7 * part // 2)
    for at, ref in zip(rows, (near_ref, first_ref, second_ref, third_ref, fourth_ref)):
        for comp in range(6):
            x = ref[:, comp].astype(jnp.float32).reshape(-1, W).astype(jnp.bfloat16)
            stations[comp, pl.ds(at, x.shape[0]), :] = x


def correlate(half, pick, stations, table, edge, out_ref, cross):
    for k in range(W // PC):
        at = k * PC
        r, s = [], []
        for comp in range(6):
            x = jnp.dot(pick[half], stations[comp, :, at : at + PC], preferred_element_type=jnp.float32)
            r.append(x[:HALF])
            s.append(x[HALF:])
        for a in range(3):
            for b in range(3):
                r0 = (3 * a + b) * HALF
                re = s[a] * r[b] + s[3 + a] * r[3 + b]
                im = s[a] * r[3 + b] - s[3 + a] * r[b]
                cross[r0 : r0 + HALF, at : at + PC] = re.astype(jnp.bfloat16)
                cross[r0 : r0 + HALF, W + at : W + at + PC] = im.astype(jnp.bfloat16)

    for n in range(NX):
        odd, at = n // 2 * W, n % 2 * TW
        part = cross[:, odd : odd + W]
        out = jnp.dot(part, table[odd : odd + W, at : at + TW], preferred_element_type=jnp.float32)
        if n == 2:
            low = out[:, :CH] + jnp.dot(cross[:, :W], edge[...], preferred_element_type=jnp.float32)
            out = jnp.concatenate([low, out[:, CH:]], axis=1)
        for c in range(9):
            for k in range(NY):
                r0 = c * HALF + k * PD
                out_ref[k, n, c] = out[r0 : r0 + PD].astype(out_ref.dtype)


def unfold(scale_ref, x_ref, out_ref):
    x = x_ref[...].reshape(9 * PD, LAGS)
    even, odd = x[:, :TN], x[:, TN:]
    turn = lax.broadcasted_iota(jnp.int32, (TN, TN), 0) + lax.broadcasted_iota(jnp.int32, (TN, TN), 1) == TN
    turn = turn.astype(jnp.float32).astype(jnp.bfloat16)
    back = jnp.dot(even, turn, preferred_element_type=jnp.float32) - jnp.dot(odd, turn, preferred_element_type=jnp.float32)
    even, odd = even.astype(jnp.float32), odd.astype(jnp.float32)
    zero = lax.broadcasted_iota(jnp.int32, (9 * PD, TN), 1) == 0
    back = jnp.where(zero, odd, back) * scale_ref[:, :TN]
    ahead = jnp.where(zero, even, even + odd) * scale_ref[:, TN:]
    out_ref[:, :, :TN] = back.reshape(9, PD, TN)
    out_ref[:, :, TN:] = ahead.reshape(9, PD, TN)


def vmem(n):
    return [pl.BlockSpec(memory_space=pltpu.VMEM)] * n


def body(spectra, pair_source, pair_owner, pair_row):
    s, g = lax.axis_index("sta"), lax.axis_index("grp")
    mine = lax.dynamic_slice_in_dim(spectra[0], g * W, W, 2).transpose(1, 0, 2)
    planes = [list(range(p, NZ, NR)) for p in range(NR)]
    near = lax.all_gather(mine, "sta", axis=0, axis_index_groups=planes)

    def neighbour(x, step):
        turn = [step if i % NC == 0 else -step for i in range(NG)]
        perm = [(z * NG + i, (z + turn[i]) % NZ * NG + i) for z in range(NZ) for i in range(NG)]
        return lax.ppermute(x, ("sta", "grp"), perm)

    pos = jnp.arange(LAGS, dtype=jnp.float32)[None]
    taper = 0.75 - 0.25 * jnp.cos(TWO_PI * (pos + 0.5) / LAGS)
    scale = taper / (NX * math.sqrt(NB))
    half = NZ // NR // 2
    low, high, pair_row = lax.optimization_barrier((near[:half], near[half:], pair_row))
    moved = (neighbour(near, 1), neighbour(near, -1), neighbour(low, 2), neighbour(high, -2))

    smem = pl.BlockSpec(memory_space=pltpu.SMEM)
    code = pl.pallas_call(
        codes,
        out_shape=jax.ShapeDtypeStruct((NG, PD), jnp.int32),
        in_specs=[smem] + vmem(3),
        out_specs=vmem(1)[0],
        cost_estimate=pl.CostEstimate(flops=10**10, bytes_accessed=10**6, transcendentals=0),
        name="codes",
    )(s[None], pair_source[None], pair_owner.T, pair_row[None])
    code = lax.all_to_all(code, "grp", 0, 0, tiled=True)
    code, moved, scale = lax.optimization_barrier((code, moved, scale))

    params = pltpu.CompilerParams(vmem_limit_bytes=VMEM_LIMIT)
    table, edge, stations, pick = pl.pallas_call(
        stage,
        out_shape=(
            jax.ShapeDtypeStruct((2 * W, TN), jnp.bfloat16),
            jax.ShapeDtypeStruct((W, CH), jnp.bfloat16),
            jax.ShapeDtypeStruct((6, NZ * SD, W), jnp.bfloat16),
            jax.ShapeDtypeStruct((NC, 2 * HALF, NZ * SD), jnp.bfloat16),
        ),
        in_specs=[smem] + vmem(6),
        out_specs=tuple(vmem(4)),
        scratch_shapes=[
            pltpu.VMEM((8, NC * 2 * HALF), jnp.int32),
            pltpu.VMEM((FINE, TA), jnp.float32),
            pltpu.VMEM((FINE, TA), jnp.float32),
        ],
        compiler_params=params,
        name="stage",
    )(g[None], code, near, *moved)

    def lags(half, dtype):
        return pl.pallas_call(
            functools.partial(correlate, half),
            out_shape=jax.ShapeDtypeStruct((NY, NX, 9, PD, TW), dtype),
            in_specs=vmem(4),
            out_specs=vmem(1)[0],
            scratch_shapes=[pltpu.VMEM((9 * HALF, 2 * W), jnp.bfloat16)],
            compiler_params=params,
            name="correlate",
        )(pick, stations, table, edge)

    send = lags(0, jnp.bfloat16)
    keep = lags(1, jnp.float32)
    part = keep + lax.ppermute(send, "grp", [(i, i ^ 1) for i in range(NG)]).astype(jnp.float32)
    part = part.astype(jnp.bfloat16).reshape(NY * NX, 9, PD, TW)
    chips = [[(NC * y + c) * NX + x for y in range(NY) for x in range(NX)] for c in range(NC)]
    part = lax.all_to_all(part, ("grp", "hr"), 0, 0, axis_index_groups=chips, tiled=True)
    total = jnp.sum(part.astype(jnp.float32), axis=0).astype(jnp.bfloat16)
    total = lax.all_gather(total, "hr", axis=2, tiled=True)
    return pl.pallas_call(
        unfold,
        out_shape=jax.ShapeDtypeStruct((9, PD, LAGS), jnp.float32),
        in_specs=vmem(2),
        out_specs=vmem(1)[0],
        compiler_params=params,
        name="unfold",
    )(scale, total).transpose(1, 0, 2)


def solution(mesh):
    placed = (
        P("hr", "sta", None, None),
        P(("sta", "grp")),
        P(("sta", "grp"), None),
        P(("sta", "grp")),
    )
    return jax.shard_map(
        body, mesh=mesh, in_specs=placed, out_specs=P(("sta", "grp"), None, None), check_vma=False
    )
```

```python
import functools
import math

import jax
import jax.numpy as jnp
from jax import lax
from jax.experimental import pallas as pl
from jax.experimental.pallas import tpu as pltpu
from jax.sharding import PartitionSpec as P

LAGS = 1024
NZ, NG, NY, NC, NX = 16, 8, 4, 2, 4
SD, PD, NB = 8, 16, 8192
W = NB // NG
NR = 4
BITS = 10
FINE = 32
HALF = NY * PD
CH = 128
PC = 256
TN = LAGS // 2
TA = TN + CH
TW = LAGS // NX
TWO_PI = 2.0 * math.pi
VMEM_LIMIT = 24 * 1024 * 1024


def codes(plane_ref, source_ref, owner_ref, row_ref, out_ref):
    plane, owner = plane_ref[0], owner_ref[...]
    away = (owner - plane) & (NR - 1)
    first = jnp.where(away == 0, 0, jnp.where(away == 3, 1, jnp.where(away == 1, 2, 3)))
    slot = first * (NZ // NR) + owner // NR
    code = (slot * SD + row_ref[...]) * (NZ * SD) + plane // NR * SD + source_ref[...]
    out_ref[...] = jnp.broadcast_to(code, (NG, PD))


def stage(grp_ref, code_ref, near_ref, first_ref, second_ref, third_ref, fourth_ref, table, edge, stations, pick, row, hi_c, hi_s):
    core, g = grp_ref[0] % NC, grp_ref[0]
    bit = lax.broadcasted_iota(jnp.int32, (16, TA), 0)
    lag = jnp.minimum(lax.broadcasted_iota(jnp.int32, (16, TA), 1), TN)
    bins = jnp.where(bit < BITS, jnp.left_shift(1, bit), g * W)
    ang = ((bins * lag) & (2 * NB - 1)).astype(jnp.float32) * (TWO_PI / (2 * NB))
    cos, sin = jnp.cos(ang), jnp.sin(ang)

    def turned(c, s, bits):
        at = lax.broadcasted_iota(jnp.int32, (FINE, TA), 0)
        for k, b in enumerate(bits):
            on = (jnp.right_shift(at, k) & 1) == 1
            kc, ks = jnp.where(on, cos[b : b + 1], 1.0), jnp.where(on, sin[b : b + 1], 0.0)
            c, s = c * kc - s * ks, s * kc + c * ks
        return c, s

    half_bits = BITS // 2
    lc, ls = turned(jnp.ones((FINE, TA), jnp.float32), jnp.zeros((FINE, TA), jnp.float32), range(half_bits))
    base = jnp.broadcast_to(cos[BITS : BITS + 1], (FINE, TA)), jnp.broadcast_to(sin[BITS : BITS + 1], (FINE, TA))
    hi_c[...], hi_s[...] = turned(*base, range(half_bits, BITS))

    zero = lax.broadcasted_iota(jnp.int32, (FINE, CH), 1) == 0

    def fill(i, carry):
        hc, hs = hi_c[pl.ds(i, 1), :], hi_s[pl.ds(i, 1), :]
        at = pl.multiple_of(i * FINE, FINE)
        c, s = hc * lc - hs * ls, hs * lc + hc * ls
        table[pl.ds(at, FINE), :] = c[:, :TN].astype(jnp.bfloat16)
        table[pl.ds(W + at, FINE), :] = (-s[:, :TN]).astype(jnp.bfloat16)
        table[pl.ds(W + at, FINE), 0:CH] = jnp.where(zero, s[:, TN:], -s[:, :CH]).astype(jnp.bfloat16)
        edge[pl.ds(at, FINE), :] = jnp.where(zero, c[:, TN:], 0.0).astype(jnp.bfloat16)
        return carry

    lax.fori_loop(0, W // FINE, fill, 0)

    even = core == 0
    for k in range(NY):
        c0, c1 = code_ref[NC * k : NC * k + 1], code_ref[NC * k + 1 : NC * k + 2]
        for half, code in enumerate((jnp.where(even, c1, c0), jnp.where(even, c0, c1))):
            at = half * 2 * HALF + k * PD
            row[0:1, at : at + PD] = code // (NZ * SD)
            row[0:1, at + HALF : at + HALF + PD] = code % (NZ * SD)
    station = lax.broadcasted_iota(jnp.int32, (NZ * SD, 2 * HALF), 0)
    for half in range(NC):
        hot = (station == row[0:1, half * 2 * HALF : (half + 1) * 2 * HALF]).astype(jnp.float32)
        pick[half] = hot.T.astype(jnp.bfloat16)
    part = NZ * SD // NR
    rows = (0, pl.multiple_of(part + core * part, part), pl.multiple_of(2 * part - core * part, part), 3 * part, 7 * part // 2)
    for at, ref in zip(rows, (near_ref, first_ref, second_ref, third_ref, fourth_ref)):
        for comp in range(6):
            x = ref[:, comp].astype(jnp.float32).reshape(-1, W).astype(jnp.bfloat16)
            stations[comp, pl.ds(at, x.shape[0]), :] = x


def correlate(half, pick, stations, table, edge, out_ref, cross):
    for k in range(W // PC):
        at = k * PC
        r, s = [], []
        for comp in range(6):
            x = jnp.dot(pick[half], stations[comp, :, at : at + PC], preferred_element_type=jnp.float32)
            r.append(x[:HALF])
            s.append(x[HALF:])
        for a in range(3):
            for b in range(3):
                r0 = (3 * a + b) * HALF
                re = s[a] * r[b] + s[3 + a] * r[3 + b]
                im = s[a] * r[3 + b] - s[3 + a] * r[b]
                cross[r0 : r0 + HALF, at : at + PC] = re.astype(jnp.bfloat16)
                cross[r0 : r0 + HALF, W + at : W + at + PC] = im.astype(jnp.bfloat16)

    for n in range(NX):
        odd, at = n // 2 * W, n % 2 * TW
        part = cross[:, odd : odd + W]
        out = jnp.dot(part, table[odd : odd + W, at : at + TW], preferred_element_type=jnp.float32)
        if n == 2:
            low = out[:, :CH] + jnp.dot(cross[:, :W], edge[...], preferred_element_type=jnp.float32)
            out = jnp.concatenate([low, out[:, CH:]], axis=1)
        for c in range(9):
            for k in range(NY):
                r0 = c * HALF + k * PD
                out_ref[k, n, c] = out[r0 : r0 + PD].astype(out_ref.dtype)


def unfold(scale_ref, x_ref, out_ref):
    x = x_ref[...].reshape(9 * PD, LAGS)
    even, odd = x[:, :TN], x[:, TN:]
    turn = lax.broadcasted_iota(jnp.int32, (TN, TN), 0) + lax.broadcasted_iota(jnp.int32, (TN, TN), 1) == TN
    turn = turn.astype(jnp.float32).astype(jnp.bfloat16)
    back = jnp.dot(even, turn, preferred_element_type=jnp.float32) - jnp.dot(odd, turn, preferred_element_type=jnp.float32)
    even, odd = even.astype(jnp.float32), odd.astype(jnp.float32)
    zero = lax.broadcasted_iota(jnp.int32, (9 * PD, TN), 1) == 0
    back = jnp.where(zero, odd, back) * scale_ref[:, :TN]
    ahead = jnp.where(zero, even, even + odd) * scale_ref[:, TN:]
    out_ref[:, :, :TN] = back.reshape(9, PD, TN)
    out_ref[:, :, TN:] = ahead.reshape(9, PD, TN)


def vmem(n):
    return [pl.BlockSpec(memory_space=pltpu.VMEM)] * n


def body(spectra, pair_source, pair_owner, pair_row):
    s, g = lax.axis_index("sta"), lax.axis_index("grp")
    smem = pl.BlockSpec(memory_space=pltpu.SMEM)
    code = pl.pallas_call(
        codes,
        out_shape=jax.ShapeDtypeStruct((NG, PD), jnp.int32),
        in_specs=[smem] + vmem(3),
        out_specs=vmem(1)[0],
        name="codes",
    )(s[None], pair_source[None], pair_owner.T, pair_row[None])

    spectra, code = lax.optimization_barrier((spectra, code))
    mine = lax.dynamic_slice_in_dim(spectra[0], g * W, W, 2).transpose(1, 0, 2)
    planes = [list(range(p, NZ, NR)) for p in range(NR)]
    near = lax.all_gather(mine, "sta", axis=0, axis_index_groups=planes)

    def neighbour(x, step):
        turn = [step if i % NC == 0 else -step for i in range(NG)]
        perm = [(z * NG + i, (z + turn[i]) % NZ * NG + i) for z in range(NZ) for i in range(NG)]
        return lax.ppermute(x, ("sta", "grp"), perm)

    pos = jnp.arange(LAGS, dtype=jnp.float32)[None]
    taper = 0.75 - 0.25 * jnp.cos(TWO_PI * (pos + 0.5) / LAGS)
    scale = taper / (NX * math.sqrt(NB))
    half = NZ // NR // 2
    low, high, code = lax.optimization_barrier((near[:half], near[half:], code))
    moved = (neighbour(near, 1), neighbour(near, -1), neighbour(low, 2), neighbour(high, -2))
    code = lax.all_to_all(code, "grp", 0, 0, tiled=True)
    code, moved, scale = lax.optimization_barrier((code, moved, scale))

    params = pltpu.CompilerParams(vmem_limit_bytes=VMEM_LIMIT)
    table, edge, stations, pick = pl.pallas_call(
        stage,
        out_shape=(
            jax.ShapeDtypeStruct((2 * W, TN), jnp.bfloat16),
            jax.ShapeDtypeStruct((W, CH), jnp.bfloat16),
            jax.ShapeDtypeStruct((6, NZ * SD, W), jnp.bfloat16),
            jax.ShapeDtypeStruct((NC, 2 * HALF, NZ * SD), jnp.bfloat16),
        ),
        in_specs=[smem] + vmem(6),
        out_specs=tuple(vmem(4)),
        scratch_shapes=[
            pltpu.VMEM((8, NC * 2 * HALF), jnp.int32),
            pltpu.VMEM((FINE, TA), jnp.float32),
            pltpu.VMEM((FINE, TA), jnp.float32),
        ],
        compiler_params=params,
        name="stage",
    )(g[None], code, near, *moved)

    def lags(half, dtype):
        return pl.pallas_call(
            functools.partial(correlate, half),
            out_shape=jax.ShapeDtypeStruct((NY, NX, 9, PD, TW), dtype),
            in_specs=vmem(4),
            out_specs=vmem(1)[0],
            scratch_shapes=[pltpu.VMEM((9 * HALF, 2 * W), jnp.bfloat16)],
            compiler_params=params,
            name="correlate",
        )(pick, stations, table, edge)

    send = lags(0, jnp.bfloat16)
    keep = lags(1, jnp.float32)
    part = keep + lax.ppermute(send, "grp", [(i, i ^ 1) for i in range(NG)]).astype(jnp.float32)
    part = part.astype(jnp.bfloat16).reshape(NY * NX, 9, PD, TW)
    chips = [[(NC * y + c) * NX + x for y in range(NY) for x in range(NX)] for c in range(NC)]
    part = lax.all_to_all(part, ("grp", "hr"), 0, 0, axis_index_groups=chips, tiled=True)
    total = jnp.sum(part.astype(jnp.float32), axis=0).astype(jnp.bfloat16)
    total = lax.all_gather(total, "hr", axis=2, tiled=True)
    return pl.pallas_call(
        unfold,
        out_shape=jax.ShapeDtypeStruct((9, PD, LAGS), jnp.float32),
        in_specs=vmem(2),
        out_specs=vmem(1)[0],
        compiler_params=params,
        name="unfold",
    )(scale, total).transpose(1, 0, 2)


def solution(mesh):
    placed = (
        P("hr", "sta", None, None),
        P(("sta", "grp")),
        P(("sta", "grp"), None),
        P(("sta", "grp")),
    )
    return jax.shard_map(
        body, mesh=mesh, in_specs=placed, out_specs=P(("sta", "grp"), None, None), check_vma=False
    )
```

```python
import functools
import math

import jax
import jax.numpy as jnp
from jax import lax
from jax.experimental import pallas as pl
from jax.experimental.pallas import tpu as pltpu
from jax.sharding import PartitionSpec as P

LAGS = 1024
NZ, NG, NY, NC, NX = 16, 8, 4, 2, 4
SD, PD, NB = 8, 16, 8192
W = NB // NG
NR = 4
BITS = 10
FINE = 32
HALF = NY * PD
CH = 128
PC = 512
TN = LAGS // 2
TA = TN + CH
TW = LAGS // NX
TWO_PI = 2.0 * math.pi
VMEM_LIMIT = 24 * 1024 * 1024


def codes(plane_ref, source_ref, owner_ref, row_ref, out_ref):
    plane, owner = plane_ref[0], owner_ref[...]
    away = (owner - plane) & (NR - 1)
    first = jnp.where(away == 0, 0, jnp.where(away == 3, 1, jnp.where(away == 1, 2, 3)))
    slot = first * (NZ // NR) + owner // NR
    code = (slot * SD + row_ref[...]) * (NZ * SD) + plane // NR * SD + source_ref[...]
    out_ref[...] = jnp.broadcast_to(code, (NG, PD))


def stage(grp_ref, code_ref, near_ref, first_ref, second_ref, third_ref, fourth_ref, table, edge, stations, pick, row, hi_c, hi_s):
    core, g = grp_ref[0] % NC, grp_ref[0]
    bit = lax.broadcasted_iota(jnp.int32, (16, TA), 0)
    lag = jnp.minimum(lax.broadcasted_iota(jnp.int32, (16, TA), 1), TN)
    bins = jnp.where(bit < BITS, jnp.left_shift(1, bit), g * W)
    ang = ((bins * lag) & (2 * NB - 1)).astype(jnp.float32) * (TWO_PI / (2 * NB))
    cos, sin = jnp.cos(ang), jnp.sin(ang)

    def turned(c, s, bits):
        at = lax.broadcasted_iota(jnp.int32, (FINE, TA), 0)
        for k, b in enumerate(bits):
            on = (jnp.right_shift(at, k) & 1) == 1
            kc, ks = jnp.where(on, cos[b : b + 1], 1.0), jnp.where(on, sin[b : b + 1], 0.0)
            c, s = c * kc - s * ks, s * kc + c * ks
        return c, s

    half_bits = BITS // 2
    lc, ls = turned(jnp.ones((FINE, TA), jnp.float32), jnp.zeros((FINE, TA), jnp.float32), range(half_bits))
    base = jnp.broadcast_to(cos[BITS : BITS + 1], (FINE, TA)), jnp.broadcast_to(sin[BITS : BITS + 1], (FINE, TA))
    hi_c[...], hi_s[...] = turned(*base, range(half_bits, BITS))

    zero = lax.broadcasted_iota(jnp.int32, (FINE, CH), 1) == 0

    def fill(i, carry):
        hc, hs = hi_c[pl.ds(i, 1), :], hi_s[pl.ds(i, 1), :]
        at = pl.multiple_of(i * FINE, FINE)
        c, s = hc * lc - hs * ls, hs * lc + hc * ls
        table[pl.ds(at, FINE), :] = c[:, :TN].astype(jnp.bfloat16)
        table[pl.ds(W + at, FINE), :] = (-s[:, :TN]).astype(jnp.bfloat16)
        table[pl.ds(W + at, FINE), 0:CH] = jnp.where(zero, s[:, TN:], -s[:, :CH]).astype(jnp.bfloat16)
        edge[pl.ds(at, FINE), :] = jnp.where(zero, c[:, TN:], 0.0).astype(jnp.bfloat16)
        return carry

    lax.fori_loop(0, W // FINE, fill, 0)

    even = core == 0
    for k in range(NY):
        c0, c1 = code_ref[NC * k : NC * k + 1], code_ref[NC * k + 1 : NC * k + 2]
        for half, code in enumerate((jnp.where(even, c1, c0), jnp.where(even, c0, c1))):
            at = half * 2 * HALF + k * PD
            row[0:1, at : at + PD] = code // (NZ * SD)
            row[0:1, at + HALF : at + HALF + PD] = code % (NZ * SD)
    station = lax.broadcasted_iota(jnp.int32, (NZ * SD, 2 * HALF), 0)
    for half in range(NC):
        hot = (station == row[0:1, half * 2 * HALF : (half + 1) * 2 * HALF]).astype(jnp.float32)
        pick[half] = hot.T.astype(jnp.bfloat16)
    part = NZ * SD // NR
    rows = (0, pl.multiple_of(part + core * part, part), pl.multiple_of(2 * part - core * part, part), 3 * part, 7 * part // 2)
    for at, ref in zip(rows, (near_ref, first_ref, second_ref, third_ref, fourth_ref)):
        for comp in range(6):
            x = ref[:, comp].astype(jnp.float32).reshape(-1, W).astype(jnp.bfloat16)
            stations[comp, pl.ds(at, x.shape[0]), :] = x


def correlate(half, pick, stations, table, edge, out_ref, cross):
    for k in range(W // PC):
        at = k * PC
        r, s = [], []
        for comp in range(6):
            x = jnp.dot(pick[half], stations[comp, :, at : at + PC], preferred_element_type=jnp.float32)
            r.append(x[:HALF])
            s.append(x[HALF:])
        for a in range(3):
            for b in range(3):
                r0 = (3 * a + b) * HALF
                re = s[a] * r[b] + s[3 + a] * r[3 + b]
                im = s[a] * r[3 + b] - s[3 + a] * r[b]
                cross[r0 : r0 + HALF, at : at + PC] = re.astype(jnp.bfloat16)
                cross[r0 : r0 + HALF, W + at : W + at + PC] = im.astype(jnp.bfloat16)

    for n in range(NX):
        odd, at = n // 2 * W, n % 2 * TW
        part = cross[:, odd : odd + W]
        out = jnp.dot(part, table[odd : odd + W, at : at + TW], preferred_element_type=jnp.float32)
        if n == 2:
            low = out[:, :CH] + jnp.dot(cross[:, :W], edge[...], preferred_element_type=jnp.float32)
            out = jnp.concatenate([low, out[:, CH:]], axis=1)
        for c in range(9):
            for k in range(NY):
                r0 = c * HALF + k * PD
                out_ref[k, n, c] = out[r0 : r0 + PD].astype(out_ref.dtype)


def unfold(scale_ref, x_ref, out_ref):
    x = x_ref[...].reshape(9 * PD, LAGS)
    even, odd = x[:, :TN], x[:, TN:]
    turn = lax.broadcasted_iota(jnp.int32, (TN, TN), 0) + lax.broadcasted_iota(jnp.int32, (TN, TN), 1) == TN
    turn = turn.astype(jnp.float32).astype(jnp.bfloat16)
    back = jnp.dot(even, turn, preferred_element_type=jnp.float32) - jnp.dot(odd, turn, preferred_element_type=jnp.float32)
    even, odd = even.astype(jnp.float32), odd.astype(jnp.float32)
    zero = lax.broadcasted_iota(jnp.int32, (9 * PD, TN), 1) == 0
    back = jnp.where(zero, odd, back) * scale_ref[:, :TN]
    ahead = jnp.where(zero, even, even + odd) * scale_ref[:, TN:]
    out_ref[:, :, :TN] = back.reshape(9, PD, TN)
    out_ref[:, :, TN:] = ahead.reshape(9, PD, TN)


def vmem(n):
    return [pl.BlockSpec(memory_space=pltpu.VMEM)] * n


def body(spectra, pair_source, pair_owner, pair_row):
    s, g = lax.axis_index("sta"), lax.axis_index("grp")
    smem = pl.BlockSpec(memory_space=pltpu.SMEM)
    code = pl.pallas_call(
        codes,
        out_shape=jax.ShapeDtypeStruct((NG, PD), jnp.int32),
        in_specs=[smem] + vmem(3),
        out_specs=vmem(1)[0],
        name="codes",
    )(s[None], pair_source[None], pair_owner.T, pair_row[None])

    spectra, code = lax.optimization_barrier((spectra, code))
    mine = lax.dynamic_slice_in_dim(spectra[0], g * W, W, 2).transpose(1, 0, 2)
    planes = [list(range(p, NZ, NR)) for p in range(NR)]
    near = lax.all_gather(mine, "sta", axis=0, axis_index_groups=planes)

    def neighbour(x, step):
        turn = [step if i % NC == 0 else -step for i in range(NG)]
        perm = [(z * NG + i, (z + turn[i]) % NZ * NG + i) for z in range(NZ) for i in range(NG)]
        return lax.ppermute(x, ("sta", "grp"), perm)

    pos = jnp.arange(LAGS, dtype=jnp.float32)[None]
    taper = 0.75 - 0.25 * jnp.cos(TWO_PI * (pos + 0.5) / LAGS)
    scale = taper / (NX * math.sqrt(NB))
    half = NZ // NR // 2
    low, high, code = lax.optimization_barrier((near[:half], near[half:], code))
    moved = (neighbour(near, 1), neighbour(near, -1), neighbour(low, 2), neighbour(high, -2))
    code = lax.all_to_all(code, "grp", 0, 0, tiled=True)
    code, moved, scale = lax.optimization_barrier((code, moved, scale))

    params = pltpu.CompilerParams(vmem_limit_bytes=VMEM_LIMIT)
    table, edge, stations, pick = pl.pallas_call(
        stage,
        out_shape=(
            jax.ShapeDtypeStruct((2 * W, TN), jnp.bfloat16),
            jax.ShapeDtypeStruct((W, CH), jnp.bfloat16),
            jax.ShapeDtypeStruct((6, NZ * SD, W), jnp.bfloat16),
            jax.ShapeDtypeStruct((NC, 2 * HALF, NZ * SD), jnp.bfloat16),
        ),
        in_specs=[smem] + vmem(6),
        out_specs=tuple(vmem(4)),
        scratch_shapes=[
            pltpu.VMEM((8, NC * 2 * HALF), jnp.int32),
            pltpu.VMEM((FINE, TA), jnp.float32),
            pltpu.VMEM((FINE, TA), jnp.float32),
        ],
        compiler_params=params,
        name="stage",
    )(g[None], code, near, *moved)

    def lags(half, dtype):
        return pl.pallas_call(
            functools.partial(correlate, half),
            out_shape=jax.ShapeDtypeStruct((NY, NX, 9, PD, TW), dtype),
            in_specs=vmem(4),
            out_specs=vmem(1)[0],
            scratch_shapes=[pltpu.VMEM((9 * HALF, 2 * W), jnp.bfloat16)],
            compiler_params=params,
            name="correlate",
        )(pick, stations, table, edge)

    send = lags(0, jnp.bfloat16)
    keep = lags(1, jnp.float32)
    part = keep + lax.ppermute(send, "grp", [(i, i ^ 1) for i in range(NG)]).astype(jnp.float32)
    part = part.astype(jnp.bfloat16).reshape(NY * NX, 9, PD, TW)
    chips = [[(NC * y + c) * NX + x for y in range(NY) for x in range(NX)] for c in range(NC)]
    part = lax.all_to_all(part, ("grp", "hr"), 0, 0, axis_index_groups=chips, tiled=True)
    total = jnp.sum(part.astype(jnp.float32), axis=0).astype(jnp.bfloat16)
    total = lax.all_gather(total, "hr", axis=2, tiled=True)
    return pl.pallas_call(
        unfold,
        out_shape=jax.ShapeDtypeStruct((9, PD, LAGS), jnp.float32),
        in_specs=vmem(2),
        out_specs=vmem(1)[0],
        compiler_params=params,
        name="unfold",
    )(scale, total).transpose(1, 0, 2)


def solution(mesh):
    placed = (
        P("hr", "sta", None, None),
        P(("sta", "grp")),
        P(("sta", "grp"), None),
        P(("sta", "grp")),
    )
    return jax.shard_map(
        body, mesh=mesh, in_specs=placed, out_specs=P(("sta", "grp"), None, None), check_vma=False
    )
```
